512 devices in a mesh: leaf: 64 (over y, z), front: 8 (over x, core).
Axes of the slice: x: 4, y: 4, z: 16, core: 2. Of those that a mesh axis runs over, the one named last changes fastest.
Arguments:
- rhs: float32 [5, 2, 16, 20480], P(None, None, None, ('leaf', 'front')), may hold values from -6 to 6
- inv_blocks: bfloat16 [2, 20480, 19840], P(None, 'leaf', 'front'), may hold values from -1 to 1
- upd_blocks: bfloat16 [2, 20480, 9600], P(None, 'leaf', 'front'), may hold values from -1 to 1
- tile_mask: int32 [64, 30], P('leaf'), may hold values 0 or 1
Outputs:
- solution: float32 [5, 2, 16, 20480], P(None, None, None, ('leaf', 'front'))
The draws below stay inside these ranges and needn't reach their ends.
All inputs are finite; a program needn't handle non-finite values. No bound on the sum of `tile_mask` on one device may be relied on, other than what follows from the above.
Results may differ from the reference program's by a relative error of at most 0.007.
Values may be sent and summed in bfloat16 or wider, within the bound.
No kernel may reach another device: no remote copies, remote signals or barrier semaphores. Data moves between devices by JAX's collectives and lax.ppermute only.
A program may use at most 64 MiB of HBM per device.

```python
import jax
import jax.numpy as jnp
from jax import lax

R = 320
RHS = 16
BLOCKS = 64
LEVELS = 5
RP = 40
SEP_ROWS = 20480
MASK_COLS = 30
N_FRONT = 8


def column_scale(total_cols, groups, first_level, upper_end):
    position = jnp.arange(total_cols) % (groups * RP)
    group_id = position // RP
    col_scale = jnp.zeros((total_cols,), jnp.float32)
    for height in range(first_level, LEVELS):
        members = BLOCKS >> height + 1
        inside = (group_id >= upper_end - 2 * members) & (group_id < upper_end - members)
        col_scale = col_scale + jnp.where(inside, (2 * members * R) ** (-0.5), 0.0)
    return col_scale


def factor_draw(key, row_count, total_cols, groups, first_level, upper_end):
    col_scale = column_scale(total_cols, groups, first_level, upper_end)
    entries = jnp.clip(jax.random.normal(key, (2, row_count, total_cols), jnp.float32), -4.0, 4.0)
    return (entries * col_scale[None, None, :]).astype(jnp.bfloat16)


def draw_inv_blocks(key, part):
    return factor_draw(jax.random.fold_in(key, 11), BLOCKS * R, (BLOCKS - 2) * R, BLOCKS - 2, 0, BLOCKS)


def draw_upd_blocks(key, part):
    return factor_draw(jax.random.fold_in(key, 23), BLOCKS * R, (BLOCKS // 2 - 2) * R, BLOCKS // 2 - 2, 1, BLOCKS // 2)


def plant(values, own_key, smallest, high):
    longest = values.shape.index(max(values.shape))
    spots = []
    for shift in (0, 1):
        where = [jax.random.randint(jax.random.fold_in(own_key, axis), (), 0, length) for axis, length in enumerate(values.shape)]
        where[longest] = (where[longest] + shift) % values.shape[longest]
        spots.append(tuple(where))
    return values.at[spots[0]].set(smallest).at[spots[1]].set(high)


def levels(key, shape, cuts, least, largest):
    loudness, own = 1.0, jax.random.fold_in(key, 6)
    for axis_at, blocks in cuts:
        draws = jnp.exp(jax.random.uniform(jax.random.fold_in(own, axis_at), (blocks,), jnp.float32, least / len(cuts), largest / len(cuts)))
        loudness = loudness * jnp.repeat(draws, shape[axis_at] // blocks).reshape([-1 if axis == axis_at else 1 for axis in range(len(shape))])
    return loudness


def centred(key, extent, scale, limit, split=(), dtype=jnp.bfloat16):
    values = jax.random.normal(key, extent, jnp.float32) * scale
    if len(split) > 0:
        values = levels(key, extent, split, -0.22, 0.18) * values
    return jnp.clip(values, min=-limit, max=limit).astype(dtype)


def setup_inputs(seed: int = 0) -> dict:
    key_list = jax.random.split(jax.random.key(seed), 5)
    return {
        "rhs": centred(key_list[0], (LEVELS, 2, RHS, SEP_ROWS), 1.0, 6.0, ((3, 512),), jnp.float32),
        "inv_blocks": draw_inv_blocks(jax.random.fold_in(key_list[4], 71), 0),
        "upd_blocks": draw_upd_blocks(jax.random.fold_in(key_list[4], 71), 0),
        "tile_mask": plant((jax.random.randint(key_list[3], (BLOCKS, MASK_COLS), 0, 4) < 3).astype(jnp.int32), jax.random.fold_in(key_list[3], 1), 0, 1),
    }


def apply_block(inputs, matrix):
    return jnp.einsum("rfbj,fbjai->rfai", inputs, matrix, precision=lax.Precision.HIGHEST)


def complex_apply(inputs, matrix):
    real_part = apply_block(inputs[0], matrix[0]) - apply_block(inputs[1], matrix[1])
    imag_part = apply_block(inputs[0], matrix[1]) + apply_block(inputs[1], matrix[0])
    return jnp.stack([real_part, imag_part])


def reference(rhs, inv_blocks, upd_blocks, tile_mask):
    rows_dev = R // N_FRONT
    inverse = inv_blocks.reshape(2, BLOCKS, R, N_FRONT, BLOCKS - 2, rows_dev)
    update = upd_blocks.reshape(2, BLOCKS, R, N_FRONT, BLOCKS // 2 - 2, rows_dev)
    carried = jnp.zeros((2, RHS, BLOCKS, R), jnp.float32)
    solved = []
    for height in range(LEVELS - 1, -1, -1):
        subcube = BLOCKS >> (height + 1)
        fronts = BLOCKS // subcube
        lowered = (rhs[height].reshape(2, RHS, BLOCKS, R) - carried).astype(jnp.bfloat16)
        inputs = lax.optimization_barrier(lowered).astype(jnp.float32).reshape(2, RHS, fronts, subcube, R)
        offset = BLOCKS - 2 * subcube
        pieces = []
        for column in range(N_FRONT):
            matrix = inverse[:, :, :, column, offset:offset + subcube, :].astype(jnp.float32)
            matrix = matrix.reshape(2, fronts, subcube, R, subcube, rows_dev)
            pieces.append(complex_apply(inputs, matrix))
        result = jnp.stack(pieces, axis=4).reshape(2, RHS, BLOCKS, R)
        solved.append(result)
        if height > 0:
            rounded = lax.optimization_barrier(result.astype(jnp.bfloat16)).astype(jnp.float32)
            rounded = rounded.reshape(2, RHS, fronts, subcube, R)
            upd_offset = BLOCKS // 2 - 2 * subcube
            tile_gates = tile_mask[:, upd_offset:upd_offset + subcube].astype(jnp.float32)
            tile_gates = tile_gates.reshape(fronts, subcube, subcube)
            pieces = []
            for column in range(N_FRONT):
                matrix = update[:, :, :, column, upd_offset:upd_offset + subcube, :].astype(jnp.float32)
                matrix = matrix.reshape(2, fronts, subcube, R, subcube, rows_dev)
                matrix = matrix * tile_gates[None, :, :, None, :, None]
                pieces.append(complex_apply(rounded, matrix))
            carried = jnp.stack(pieces, axis=4).reshape(2, RHS, BLOCKS, R)
    return jnp.stack(solved[::-1]).reshape(LEVELS, 2, RHS, BLOCKS * R)
```

```python
import jax
import jax.numpy as jnp
from jax import lax
from jax.experimental import pallas as pl
from jax.experimental.pallas import tpu as pltpu
from jax.sharding import Mesh
from jax.sharding import PartitionSpec as P

LEAF = ("y1", "y0", "z3", "z2", "z1", "z0")
FRONT = ("x", "core")
SPLIT = (1,)


def lane_window(columns, start, width):
    first = start // 128 * 128
    last = min(-(-(start + width) // 128) * 128, columns)
    return first, last


def whole(space=pltpu.VMEM):
    return pl.BlockSpec(memory_space=space)


def call(body, outs, inputs, scalars=0):
    specs = [whole(pltpu.SMEM)] * scalars + [whole()] * (len(inputs) - scalars)
    return pl.pallas_call(
        body,
        out_shape=outs,
        in_specs=specs,
        out_specs=jax.tree.map(lambda _: whole(), outs),
    )(*inputs)


def message(real, imag):
    return jnp.concatenate([real, imag], axis=1)


def summed_chunks(received, fronts):
    count, rows, lanes = received.shape
    parts = received[...].astype(jnp.float32).reshape(count // fronts, fronts, rows, lanes)
    return jnp.sum(parts, axis=0)


def own_chunk(chunks, own):
    total = jnp.zeros(chunks.shape[1:], jnp.float32)
    for c in range(chunks.shape[0]):
        total = total + jnp.where(own == c, chunks[c], 0.0)
    return total


def stacked_input(chunks):
    half = chunks.shape[2] // 2
    real = jnp.concatenate([c[:, :half] for c in chunks], axis=1)
    imag = jnp.concatenate([c[:, half:] for c in chunks], axis=1)
    upper = jnp.concatenate([real, -imag], axis=1)
    lower = jnp.concatenate([imag, real], axis=1)
    return jnp.concatenate([upper, lower], axis=0).astype(jnp.bfloat16)


def products(chunks, matrix, start, width):
    first, last = lane_window(matrix.shape[2], start, width)
    weights = matrix[:, :, first:last].reshape(-1, last - first)
    out = jnp.dot(stacked_input(chunks), weights, preferred_element_type=jnp.float32)
    return out, start - first


def member_message(out, shift, member, rows_dev):
    rhs_count = out.shape[0] // 2
    lane = shift + member * rows_dev
    piece = out[:, lane : lane + rows_dev]
    return message(piece[:rhs_count], piece[rhs_count:])


def put(sent, member, value, copies):
    value = value.astype(jnp.bfloat16)
    for c in range(copies):
        sent[member * copies + c] = value


def shards(rhs, inv_blocks, upd_blocks, tile_mask):
    axes = {name: lax.axis_size(name) for name in LEAF + FRONT}
    fronts = axes["x"] * axes["core"]
    blocks = 1
    for name in LEAF:
        blocks *= axes[name]
    levels, _, rhs_count, rows_dev = rhs.shape
    msg = (rhs_count, 2 * rows_dev)
    leaf = lax.axis_index(LEAF).astype(jnp.int32)
    front = lax.axis_index(FRONT).astype(jnp.int32)
    place = jnp.stack([leaf, front])
    bf16 = jnp.bfloat16

    def sent_shape(count):
        return jax.ShapeDtypeStruct((count,) + msg, bf16)

    sol_shape = jax.ShapeDtypeStruct((2, rhs_count, rows_dev), jnp.float32)

    def write_solution(sol, value):
        sol[0] = value[:, :rows_dev]
        sol[1] = value[:, rows_dev:]

    def over(value, names):
        return lax.all_to_all(value, names, 0, 0, tiled=True)

    def first_body(rhs_ref, sent):
        put(sent, 0, message(rhs_ref[levels - 1, 0], rhs_ref[levels - 1, 1]), fronts)

    def invert(level, received):
        members = blocks >> (level + 1)
        copies = 1 if level in SPLIT or level == 0 else fronts

        def body(received_ref, matrix, sent):
            chunks = summed_chunks(received_ref, fronts)
            out, shift = products(chunks, matrix, (blocks - 2 * members) * rows_dev, members * rows_dev)
            for a in range(members):
                put(sent, a, member_message(out, shift, a, rows_dev), copies)

        return call(body, sent_shape(members * copies), (received, inv_blocks))

    def update(level, received, known):
        members = blocks >> (level + 1)
        copies = 1 if level in SPLIT else fronts
        offset = blocks // 2 - 2 * members

        def body(place_ref, mask, received_ref, rhs_ref, matrix, *outs):
            sent = outs[0]
            chunks = summed_chunks(received_ref, fronts)
            if not known:
                write_solution(outs[1], own_chunk(chunks, place_ref[1]))
            out, shift = products(chunks, matrix, offset * rows_dev, members * rows_dev)
            own = place_ref[0] % members
            right = message(rhs_ref[level - 1, 0], rhs_ref[level - 1, 1])
            for a in range(members):
                gate = mask[0, offset + a].astype(jnp.float32)
                part = member_message(out, shift, a, rows_dev) * gate
                put(sent, a, jnp.where(own == a, right, 0.0) - part, copies)

        outs = (sent_shape(members * copies),) + (() if known else (sol_shape,))
        return call(body, outs, (place, tile_mask, received, rhs, upd_blocks), 2)

    def combine(received, solution):
        def body(received_ref, sent, *outs):
            total = summed_chunks(received_ref, 1)[0]
            if solution:
                write_solution(outs[0], total)
            put(sent, 0, total, fronts)

        outs = (sent_shape(fronts),) + ((sol_shape,) if solution else ())
        return call(body, outs, (received,))

    def finish(received, solved):
        def body(received_ref, *refs):
            out = refs[-1]
            write_solution(out.at[0], summed_chunks(received_ref, 1)[0])
            for level in range(1, levels):
                out[level] = refs[level - 1][...]

        return call(body, jax.ShapeDtypeStruct(rhs.shape, jnp.float32), (received, *solved))

    received = over(call(first_body, sent_shape(fronts), (rhs,)), FRONT)
    solved = [None] * levels
    for level in range(levels - 1, -1, -1):
        group = LEAF[len(LEAF) - (levels - level) :]
        sent = invert(level, received)
        if level == 0:
            return finish(over(sent, group), solved[1:])
        if level in SPLIT:
            sent, solved[level] = combine(over(sent, group), True)
            (sent,) = update(level, over(sent, FRONT), True)
            (sent,) = combine(over(sent, group), False)
            received = over(sent, FRONT)
        else:
            sent, solved[level] = update(level, over(sent, group + FRONT), False)
            received = over(sent, group + FRONT)


def solution(mesh):
    finer = Mesh(mesh.devices.reshape(2, 2, 2, 2, 2, 2, 4, 2), LEAF + FRONT)
    placed = (
        P(None, None, None, LEAF + FRONT),
        P(None, LEAF, FRONT),
        P(None, LEAF, FRONT),
        P(LEAF, None),
    )
    return jax.shard_map(
        shards,
        mesh=finer,
        in_specs=placed,
        out_specs=P(None, None, None, LEAF + FRONT),
        check_vma=False,
    )
```

```python
import jax
import jax.numpy as jnp
from jax import lax
from jax.experimental import pallas as pl
from jax.experimental.pallas import tpu as pltpu
from jax.sharding import Mesh
from jax.sharding import PartitionSpec as P

LEAF = ("y1", "y0", "z3", "z2", "z1", "z0")
FRONT = ("x", "core")
SPLIT = (1,)


def lane_window(columns, start, width):
    first = start // 128 * 128
    last = min(-(-(start + width) // 128) * 128, columns)
    return first, last


def whole(space=pltpu.VMEM):
    return pl.BlockSpec(memory_space=space)


def call(body, outs, inputs, scalars=0):
    specs = [whole(pltpu.SMEM)] * scalars + [whole()] * (len(inputs) - scalars)
    return pl.pallas_call(
        body,
        out_shape=outs,
        in_specs=specs,
        out_specs=jax.tree.map(lambda _: whole(), outs),
        compiler_params=pltpu.CompilerParams(vmem_limit_bytes=16 * 2**20),
    )(*inputs)


def message(real, imag):
    return jnp.concatenate([real, imag], axis=1)


def summed_chunks(received, fronts):
    count, rows, lanes = received.shape
    parts = received[...].astype(jnp.float32).reshape(count // fronts, fronts, rows, lanes)
    return jnp.sum(parts, axis=0)


def own_chunk(chunks, own):
    total = jnp.zeros(chunks.shape[1:], jnp.float32)
    for c in range(chunks.shape[0]):
        total = total + jnp.where(own == c, chunks[c], 0.0)
    return total


def stacked_input(chunks):
    half = chunks.shape[2] // 2
    real = jnp.concatenate([c[:, :half] for c in chunks], axis=1)
    imag = jnp.concatenate([c[:, half:] for c in chunks], axis=1)
    upper = jnp.concatenate([real, -imag], axis=1)
    lower = jnp.concatenate([imag, real], axis=1)
    return jnp.concatenate([upper, lower], axis=0).astype(jnp.bfloat16)


def products(chunks, matrix, start, width):
    first, last = lane_window(matrix.shape[2], start, width)
    weights = matrix[:, :, first:last].reshape(-1, last - first)
    out = jnp.dot(stacked_input(chunks), weights, preferred_element_type=jnp.float32)
    return out, start - first


def member_message(out, shift, member, rows_dev):
    rhs_count = out.shape[0] // 2
    lane = shift + member * rows_dev
    piece = out[:, lane : lane + rows_dev]
    return message(piece[:rhs_count], piece[rhs_count:])


def put(sent, member, value, copies):
    value = value.astype(jnp.bfloat16)
    for c in range(copies):
        sent[member * copies + c] = value


def shards(rhs, inv_blocks, upd_blocks, tile_mask):
    axes = {name: lax.axis_size(name) for name in LEAF + FRONT}
    fronts = axes["x"] * axes["core"]
    blocks = 1
    for name in LEAF:
        blocks *= axes[name]
    levels, _, rhs_count, rows_dev = rhs.shape
    msg = (rhs_count, 2 * rows_dev)
    leaf = lax.axis_index(LEAF).astype(jnp.int32)
    front = lax.axis_index(FRONT).astype(jnp.int32)
    place = jnp.stack([leaf, front])
    bf16 = jnp.bfloat16

    def sent_shape(count):
        return jax.ShapeDtypeStruct((count,) + msg, bf16)

    sol_shape = jax.ShapeDtypeStruct((2, rhs_count, rows_dev), jnp.float32)

    def write_solution(sol, value):
        sol[0] = value[:, :rows_dev]
        sol[1] = value[:, rows_dev:]

    def over(value, names):
        return lax.all_to_all(value, names, 0, 0, tiled=True)

    def first_body(rhs_ref, sent):
        put(sent, 0, message(rhs_ref[levels - 1, 0], rhs_ref[levels - 1, 1]), fronts)

    def invert(level, received):
        members = blocks >> (level + 1)
        copies = 1 if level in SPLIT or level == 0 else fronts

        def body(received_ref, matrix, sent):
            chunks = summed_chunks(received_ref, fronts)
            out, shift = products(chunks, matrix, (blocks - 2 * members) * rows_dev, members * rows_dev)
            for a in range(members):
                put(sent, a, member_message(out, shift, a, rows_dev), copies)

        return call(body, sent_shape(members * copies), (received, inv_blocks))

    def update(level, received, known):
        members = blocks >> (level + 1)
        copies = 1 if level in SPLIT else fronts
        offset = blocks // 2 - 2 * members

        def body(place_ref, mask, received_ref, rhs_ref, matrix, *outs):
            sent = outs[0]
            chunks = summed_chunks(received_ref, fronts)
            if not known:
                write_solution(outs[1], own_chunk(chunks, place_ref[1]))
            out, shift = products(chunks, matrix, offset * rows_dev, members * rows_dev)
            own = place_ref[0] % members
            right = message(rhs_ref[level - 1, 0], rhs_ref[level - 1, 1])
            for a in range(members):
                gate = mask[0, offset + a].astype(jnp.float32)
                part = member_message(out, shift, a, rows_dev) * gate
                put(sent, a, jnp.where(own == a, right, 0.0) - part, copies)

        outs = (sent_shape(members * copies),) + (() if known else (sol_shape,))
        return call(body, outs, (place, tile_mask, received, rhs, upd_blocks), 2)

    def combine(received, solution):
        def body(received_ref, sent, *outs):
            total = summed_chunks(received_ref, 1)[0]
            if solution:
                write_solution(outs[0], total)
            put(sent, 0, total, fronts)

        outs = (sent_shape(fronts),) + ((sol_shape,) if solution else ())
        return call(body, outs, (received,))

    def finish(received, solved):
        def body(received_ref, *refs):
            out = refs[-1]
            write_solution(out.at[0], summed_chunks(received_ref, 1)[0])
            for level in range(1, levels):
                out[level] = refs[level - 1][...]

        return call(body, jax.ShapeDtypeStruct(rhs.shape, jnp.float32), (received, *solved))

    received = over(call(first_body, sent_shape(fronts), (rhs,)), FRONT)
    solved = [None] * levels
    for level in range(levels - 1, -1, -1):
        group = LEAF[len(LEAF) - (levels - level) :]
        sent = invert(level, received)
        if level == 0:
            return finish(over(sent, group), solved[1:])
        if level in SPLIT:
            sent, solved[level] = combine(over(sent, group), True)
            (sent,) = update(level, over(sent, FRONT), True)
            (sent,) = combine(over(sent, group), False)
            received = over(sent, FRONT)
        else:
            sent, solved[level] = update(level, over(sent, group + FRONT), False)
            received = over(sent, group + FRONT)


def solution(mesh):
    finer = Mesh(mesh.devices.reshape(2, 2, 2, 2, 2, 2, 4, 2), LEAF + FRONT)
    placed = (
        P(None, None, None, LEAF + FRONT),
        P(None, LEAF, FRONT),
        P(None, LEAF, FRONT),
        P(LEAF, None),
    )
    return jax.shard_map(
        shards,
        mesh=finer,
        in_specs=placed,
        out_specs=P(None, None, None, LEAF + FRONT),
        check_vma=False,
    )
```

```python
import jax
import jax.numpy as jnp
from jax import lax
from jax.experimental import pallas as pl
from jax.experimental.pallas import tpu as pltpu
from jax.sharding import Mesh
from jax.sharding import PartitionSpec as P

LEAF = ("y1", "y0", "z3", "z2", "z1", "z0")
FRONT = ("x", "core")
SPLIT = (1, 2)


def lane_window(columns, start, width):
    first = start // 128 * 128
    last = min(-(-(start + width) // 128) * 128, columns)
    return first, last


def whole(space=pltpu.VMEM):
    return pl.BlockSpec(memory_space=space)


def call(body, outs, inputs):
    return pl.pallas_call(
        body,
        out_shape=outs,
        in_specs=[whole()] * len(inputs),
        out_specs=jax.tree.map(lambda _: whole(), outs),
        compiler_params=pltpu.CompilerParams(vmem_limit_bytes=16 * 2**20),
    )(*inputs)


def message(real, imag):
    return jnp.concatenate([real, imag], axis=1)


def summed_chunks(received, fronts):
    count, rows, lanes = received.shape
    parts = received[...].astype(jnp.float32).reshape(count // fronts, fronts, rows, lanes)
    return jnp.sum(parts, axis=0)


def own_chunk(chunks, own):
    total = jnp.zeros(chunks.shape[1:], jnp.float32)
    for c in range(chunks.shape[0]):
        total = total + jnp.where(own == c, chunks[c], 0.0)
    return total


def stacked_input(chunks):
    half = chunks.shape[2] // 2
    real = jnp.concatenate([c[:, :half] for c in chunks], axis=1)
    imag = jnp.concatenate([c[:, half:] for c in chunks], axis=1)
    upper = jnp.concatenate([real, -imag], axis=1)
    lower = jnp.concatenate([imag, real], axis=1)
    return jnp.concatenate([upper, lower], axis=0).astype(jnp.bfloat16)


def products(chunks, matrix, start, width):
    first, last = lane_window(matrix.shape[2], start, width)
    weights = matrix[:, :, first:last].reshape(-1, last - first)
    out = jnp.dot(stacked_input(chunks), weights, preferred_element_type=jnp.float32)
    return out, start - first


def member_message(out, shift, member, rows_dev):
    rhs_count = out.shape[0] // 2
    lane = shift + member * rows_dev
    piece = out[:, lane : lane + rows_dev]
    return message(piece[:rhs_count], piece[rhs_count:])


def put(sent, member, value, copies):
    value = value.astype(jnp.bfloat16)
    for c in range(copies):
        sent[member * copies + c] = value


def shards(rhs, inv_blocks, upd_blocks, tile_mask):
    axes = {name: lax.axis_size(name) for name in LEAF + FRONT}
    fronts = axes["x"] * axes["core"]
    blocks = 1
    for name in LEAF:
        blocks *= axes[name]
    levels, _, rhs_count, rows_dev = rhs.shape
    msg = (rhs_count, 2 * rows_dev)
    bf16 = jnp.bfloat16

    def sent_shape(count):
        return jax.ShapeDtypeStruct((count,) + msg, bf16)

    sol_shape = jax.ShapeDtypeStruct((2, rhs_count, rows_dev), jnp.float32)

    def write_solution(sol, value):
        sol[0] = value[:, :rows_dev]
        sol[1] = value[:, rows_dev:]

    def over(value, names):
        return lax.all_to_all(value, names, 0, 0, tiled=True)

    def first_body(rhs_ref, inverse, upd, sent):
        put(sent, 0, message(rhs_ref[levels - 1, 0], rhs_ref[levels - 1, 1]), fronts)

    def invert(level, received):
        members = blocks >> (level + 1)
        copies = 1 if level in SPLIT or level == 0 else fronts

        def body(received_ref, matrix, sent):
            chunks = summed_chunks(received_ref, fronts)
            out, shift = products(chunks, matrix, (blocks - 2 * members) * rows_dev, members * rows_dev)
            for a in range(members):
                put(sent, a, member_message(out, shift, a, rows_dev), copies)

        return call(body, sent_shape(members * copies), (received, inv_blocks))

    def update(level, received, known):
        members = blocks >> (level + 1)
        copies = 1 if level in SPLIT else fronts
        offset = blocks // 2 - 2 * members

        def body(mask, received_ref, rhs_ref, matrix, *outs):
            sent = outs[0]
            chunks = summed_chunks(received_ref, fronts)
            if not known:
                write_solution(outs[1], own_chunk(chunks, lax.axis_index(FRONT)))
            out, shift = products(chunks, matrix, offset * rows_dev, members * rows_dev)
            own = lax.axis_index(LEAF) % members
            gates = mask[...].astype(jnp.float32)
            right = message(rhs_ref[level - 1, 0], rhs_ref[level - 1, 1])
            for a in range(members):
                gate = gates[:, offset + a : offset + a + 1]
                part = member_message(out, shift, a, rows_dev) * gate
                put(sent, a, jnp.where(own == a, right, 0.0) - part, copies)

        outs = (sent_shape(members * copies),) + (() if known else (sol_shape,))
        return call(body, outs, (tile_mask, received, rhs, upd_blocks))

    def combine(received, solution):
        def body(received_ref, sent, *outs):
            total = summed_chunks(received_ref, 1)[0]
            if solution:
                write_solution(outs[0], total)
            put(sent, 0, total, fronts)

        outs = (sent_shape(fronts),) + ((sol_shape,) if solution else ())
        return call(body, outs, (received,))

    def finish(received, solved):
        def body(received_ref, *refs):
            out = refs[-1]
            write_solution(out.at[0], summed_chunks(received_ref, 1)[0])
            for level in range(1, levels):
                out[level] = refs[level - 1][...]

        return call(body, jax.ShapeDtypeStruct(rhs.shape, jnp.float32), (received, *solved))

    received = over(call(first_body, sent_shape(fronts), (rhs, inv_blocks, upd_blocks)), FRONT)
    solved = [None] * levels
    for level in range(levels - 1, -1, -1):
        group = LEAF[len(LEAF) - (levels - level) :]
        sent = invert(level, received)
        if level == 0:
            return finish(over(sent, group), solved[1:])
        if level in SPLIT:
            sent, solved[level] = combine(over(sent, group), True)
            (sent,) = update(level, over(sent, FRONT), True)
            (sent,) = combine(over(sent, group), False)
            received = over(sent, FRONT)
        else:
            sent, solved[level] = update(level, over(sent, group + FRONT), False)
            received = over(sent, group + FRONT)


def solution(mesh):
    finer = Mesh(mesh.devices.reshape(2, 2, 2, 2, 2, 2, 4, 2), LEAF + FRONT)
    placed = (
        P(None, None, None, LEAF + FRONT),
        P(None, LEAF, FRONT),
        P(None, LEAF, FRONT),
        P(LEAF, None),
    )
    return jax.shard_map(
        shards,
        mesh=finer,
        in_specs=placed,
        out_specs=P(None, None, None, LEAF + FRONT),
        check_vma=False,
    )
```

```python
import jax
import jax.numpy as jnp
from jax import lax
from jax.experimental import pallas as pl
from jax.experimental.pallas import tpu as pltpu
from jax.sharding import Mesh
from jax.sharding import PartitionSpec as P

LEAF = ("y1", "y0", "z3", "z2", "z1", "z0")
FRONT = ("x", "core")
SPLIT = (1, 2)


def lane_window(columns, start, width):
    first = start // 128 * 128
    last = min(-(-(start + width) // 128) * 128, columns)
    return first, last


def whole(space=pltpu.VMEM):
    return pl.BlockSpec(memory_space=space)


def call(body, outs, inputs):
    return pl.pallas_call(
        body,
        out_shape=outs,
        in_specs=[whole()] * len(inputs),
        out_specs=jax.tree.map(lambda _: whole(), outs),
        compiler_params=pltpu.CompilerParams(vmem_limit_bytes=16 * 2**20),
    )(*inputs)


def message(real, imag):
    return jnp.concatenate([real, imag], axis=1)


def summed_chunks(received, fronts):
    count, rows, lanes = received.shape
    parts = received[...].astype(jnp.float32).reshape(count // fronts, fronts, rows, lanes)
    return jnp.sum(parts, axis=0)


def own_chunk(chunks, own):
    total = jnp.zeros(chunks.shape[1:], jnp.float32)
    for c in range(chunks.shape[0]):
        total = total + jnp.where(own == c, chunks[c], 0.0)
    return total


def stacked_input(chunks):
    half = chunks.shape[2] // 2
    real = jnp.concatenate([c[:, :half] for c in chunks], axis=1)
    imag = jnp.concatenate([c[:, half:] for c in chunks], axis=1)
    upper = jnp.concatenate([real, -imag], axis=1)
    lower = jnp.concatenate([imag, real], axis=1)
    return jnp.concatenate([upper, lower], axis=0).astype(jnp.bfloat16)


def products(chunks, matrix, start, width):
    first, last = lane_window(matrix.shape[2], start, width)
    weights = matrix[:, :, first:last].reshape(-1, last - first)
    out = jnp.dot(stacked_input(chunks), weights, preferred_element_type=jnp.float32)
    return out, start - first


def member_message(out, shift, member, rows_dev):
    rhs_count = out.shape[0] // 2
    lane = shift + member * rows_dev
    piece = out[:, lane : lane + rows_dev]
    return message(piece[:rhs_count], piece[rhs_count:])


def put(sent, member, value, copies):
    value = value.astype(jnp.bfloat16)
    for c in range(copies):
        sent[member * copies + c] = value


def shards(rhs, inv_blocks, upd_blocks, tile_mask):
    axes = {name: lax.axis_size(name) for name in LEAF + FRONT}
    fronts = axes["x"] * axes["core"]
    blocks = 1
    for name in LEAF:
        blocks *= axes[name]
    levels, _, rhs_count, rows_dev = rhs.shape
    msg = (rhs_count, 2 * rows_dev)
    bf16 = jnp.bfloat16

    def sent_shape(count):
        return jax.ShapeDtypeStruct((count,) + msg, bf16)

    sol_shape = jax.ShapeDtypeStruct((2, rhs_count, rows_dev), jnp.float32)

    def write_solution(sol, value):
        sol[0] = value[:, :rows_dev]
        sol[1] = value[:, rows_dev:]

    def over(value, names):
        return lax.all_to_all(value, names, 0, 0, tiled=True)

    def first_body(rhs_ref, sent):
        put(sent, 0, message(rhs_ref[levels - 1, 0], rhs_ref[levels - 1, 1]), fronts)

    def fetch_body(inverse, upd, mask, rhs_ref, token):
        token[...] = jnp.zeros(token.shape, token.dtype)

    def invert(level, received, tokens=()):
        members = blocks >> (level + 1)
        copies = 1 if level in SPLIT or level == 0 else fronts

        def body(received_ref, matrix, *refs):
            sent = refs[-1]
            chunks = summed_chunks(received_ref, fronts)
            out, shift = products(chunks, matrix, (blocks - 2 * members) * rows_dev, members * rows_dev)
            for a in range(members):
                put(sent, a, member_message(out, shift, a, rows_dev), copies)

        return call(body, sent_shape(members * copies), (received, inv_blocks, *tokens))

    def update(level, received, known):
        members = blocks >> (level + 1)
        copies = 1 if level in SPLIT else fronts
        offset = blocks // 2 - 2 * members

        def body(mask, received_ref, rhs_ref, matrix, *outs):
            sent = outs[0]
            chunks = summed_chunks(received_ref, fronts)
            if not known:
                write_solution(outs[1], own_chunk(chunks, lax.axis_index(FRONT)))
            out, shift = products(chunks, matrix, offset * rows_dev, members * rows_dev)
            own = lax.axis_index(LEAF) % members
            gates = mask[...].astype(jnp.float32)
            right = message(rhs_ref[level - 1, 0], rhs_ref[level - 1, 1])
            for a in range(members):
                gate = gates[:, offset + a : offset + a + 1]
                part = member_message(out, shift, a, rows_dev) * gate
                put(sent, a, jnp.where(own == a, right, 0.0) - part, copies)

        outs = (sent_shape(members * copies),) + (() if known else (sol_shape,))
        return call(body, outs, (tile_mask, received, rhs, upd_blocks))

    def combine(received, solution):
        def body(received_ref, sent, *outs):
            total = summed_chunks(received_ref, 1)[0]
            if solution:
                write_solution(outs[0], total)
            put(sent, 0, total, fronts)

        outs = (sent_shape(fronts),) + ((sol_shape,) if solution else ())
        return call(body, outs, (received,))

    def finish(received, solved):
        def body(received_ref, *refs):
            out = refs[-1]
            write_solution(out.at[0], summed_chunks(received_ref, 1)[0])
            for level in range(1, levels):
                out[level] = refs[level - 1][...]

        return call(body, jax.ShapeDtypeStruct(rhs.shape, jnp.float32), (received, *solved))

    token = call(fetch_body, jax.ShapeDtypeStruct((8, 128), jnp.float32), (inv_blocks, upd_blocks, tile_mask, rhs))
    received = over(call(first_body, sent_shape(fronts), (rhs,)), FRONT)
    solved = [None] * levels
    for level in range(levels - 1, -1, -1):
        group = LEAF[len(LEAF) - (levels - level) :]
        sent = invert(level, received, (token,) if level == levels - 1 else ())
        if level == 0:
            return finish(over(sent, group), solved[1:])
        if level in SPLIT:
            sent, solved[level] = combine(over(sent, group), True)
            (sent,) = update(level, over(sent, FRONT), True)
            (sent,) = combine(over(sent, group), False)
            received = over(sent, FRONT)
        else:
            sent, solved[level] = update(level, over(sent, group + FRONT), False)
            received = over(sent, group + FRONT)


def solution(mesh):
    finer = Mesh(mesh.devices.reshape(2, 2, 2, 2, 2, 2, 4, 2), LEAF + FRONT)
    placed = (
        P(None, None, None, LEAF + FRONT),
        P(None, LEAF, FRONT),
        P(None, LEAF, FRONT),
        P(LEAF, None),
    )
    return jax.shard_map(
        shards,
        mesh=finer,
        in_specs=placed,
        out_specs=P(None, None, None, LEAF + FRONT),
        check_vma=False,
    )
```

```python
import jax
import jax.numpy as jnp
from jax import lax
from jax.experimental import pallas as pl
from jax.experimental.pallas import tpu as pltpu
from jax.sharding import Mesh
from jax.sharding import PartitionSpec as P

LEAF = ("y1", "y0", "z3", "z2", "z1", "z0")
FRONT = ("x", "core")
WITH_FRONT, THEN_FRONT, WITH_X_THEN_CORE = range(3)
WAY = {4: WITH_FRONT, 3: WITH_FRONT, 2: WITH_X_THEN_CORE, 1: THEN_FRONT}
STRIP = 4


def lane_window(columns, start, width):
    first = start // 128 * 128
    last = min(-(-(start + width) // 128) * 128, columns)
    return first, last


def whole(space=pltpu.VMEM):
    return pl.BlockSpec(memory_space=space)


def call(body, outs, inputs, space=pltpu.VMEM, scratch=()):
    return pl.pallas_call(
        body,
        out_shape=outs,
        in_specs=[whole(space)] * len(inputs),
        out_specs=jax.tree.map(lambda _: whole(), outs),
        scratch_shapes=scratch,
        compiler_params=pltpu.CompilerParams(vmem_limit_bytes=16 * 2**20),
    )(*inputs)


class Packing:
    def __init__(self, rows, lanes):
        self.rows, self.lanes = rows, lanes
        self.groups = 128 // lanes
        self.strips = -(-rows // (self.groups * STRIP))
        self.shape = (self.strips, STRIP, self.groups * lanes)

    def first_row(self, group, strip):
        return (group * self.strips + strip) * STRIP

    def pack(self, block):
        strips = []
        for j in range(self.strips):
            pieces = []
            for g in range(self.groups):
                row = self.first_row(g, j)
                if row < self.rows:
                    pieces.append(block[row : row + STRIP])
                else:
                    pieces.append(jnp.zeros((STRIP, self.lanes), jnp.float32))
            strips.append(jnp.concatenate(pieces, axis=1))
        return strips

    def unpack(self, chunks):
        rows = []
        for g in range(self.groups):
            for j in range(self.strips):
                if self.first_row(g, j) < self.rows:
                    low = g * self.lanes
                    rows.append(jnp.concatenate([c[j][:, low : low + self.lanes] for c in chunks], axis=1))
        return jnp.concatenate(rows, axis=0)


def summed_chunks(received, order):
    chunks = []
    for messages in order:
        strips = []
        for j in range(received.shape[1]):
            total = received[messages[0], j].astype(jnp.float32)
            for m in messages[1:]:
                total = total + received[m, j].astype(jnp.float32)
            strips.append(total)
        chunks.append(strips)
    return chunks


def own_chunk(chunks, own):
    strips = []
    for j in range(len(chunks[0])):
        total = jnp.zeros(chunks[0][j].shape, jnp.float32)
        for c in range(len(chunks)):
            total = total + jnp.where(own == c, chunks[c][j], 0.0)
        strips.append(total)
    return strips


def products(block, matrix, start, width):
    half = block.shape[0] // 2
    real, imag = block[:half], block[half:]
    upper = jnp.concatenate([real, -imag], axis=1)
    lower = jnp.concatenate([imag, real], axis=1)
    stacked = jnp.concatenate([upper, lower], axis=0).astype(jnp.bfloat16)
    first, last = lane_window(matrix.shape[2], start, width)
    weights = matrix[:, :, first:last].reshape(-1, last - first)
    return jnp.dot(stacked, weights, preferred_element_type=jnp.float32), start - first


def put(sent, slots, strips):
    for j, strip in enumerate(strips):
        value = strip.astype(jnp.bfloat16)
        for slot in slots:
            sent[slot, j] = value


def shards(rhs, inv_blocks, upd_blocks, tile_mask):
    axes = {name: lax.axis_size(name) for name in LEAF + FRONT}
    fronts = axes["x"] * axes["core"]
    blocks = 1
    for name in LEAF:
        blocks *= axes[name]
    levels, _, rhs_count, rows_dev = rhs.shape
    packing = Packing(2 * rhs_count, rows_dev)

    def sent_shape(count):
        return jax.ShapeDtypeStruct((count,) + packing.shape, jnp.bfloat16)

    sol_shape = jax.ShapeDtypeStruct((2, rhs_count, rows_dev), jnp.float32)

    def both_parts(rhs_ref, level):
        return jnp.concatenate([rhs_ref[level, 0], rhs_ref[level, 1]], axis=0)

    def write_solution(sol, strips):
        value = packing.unpack([strips])
        sol[0] = value[:rhs_count]
        sol[1] = value[rhs_count:]

    def over(value, names):
        return lax.all_to_all(value, names, 0, 0, tiled=True)

    def by_front(count):
        return [[m * fronts + c for m in range(count)] for c in range(fronts)]

    def copies_of(way):
        return {WITH_FRONT: fronts, WITH_X_THEN_CORE: axes["x"], THEN_FRONT: 1}[way]

    def first_body(rhs_hbm, inv_hbm, upd_hbm, mask_hbm, sent, rhs_ref, inverse, upd, mask, sems):
        pairs = ((rhs_hbm, rhs_ref), (inv_hbm, inverse), (upd_hbm, upd), (mask_hbm, mask))
        moves = [pltpu.make_async_copy(a, b, sems.at[k]) for k, (a, b) in enumerate(pairs)]
        for move in moves:
            move.start()
        moves[0].wait()
        put(sent, range(fronts), packing.pack(both_parts(rhs_ref, levels - 1)))
        for move in moves[1:]:
            move.wait()

    def same(array):
        return jax.ShapeDtypeStruct(array.shape, array.dtype)

    sent, rhs, inv_blocks, upd_blocks, tile_mask = call(
        first_body,
        (sent_shape(fronts), same(rhs), same(inv_blocks), same(upd_blocks), same(tile_mask)),
        [pltpu.with_memory_space_constraint(a, pltpu.HBM) for a in (rhs, inv_blocks, upd_blocks, tile_mask)],
        pltpu.HBM,
        (pltpu.SemaphoreType.DMA((4,)),),
    )

    def invert(level, received, order):
        members = blocks >> (level + 1)
        copies = copies_of(WAY[level]) if level > 0 else 1

        def body(received_ref, matrix, sent):
            block = packing.unpack(summed_chunks(received_ref, order))
            out, shift = products(block, matrix, (blocks - 2 * members) * rows_dev, members * rows_dev)
            for a in range(members):
                lane = shift + a * rows_dev
                strips = packing.pack(out[:, lane : lane + rows_dev])
                put(sent, range(a * copies, (a + 1) * copies), strips)

        return call(body, sent_shape(members * copies), (received, inv_blocks))

    def update(level, received, order, known):
        members = blocks >> (level + 1)
        copies = copies_of(WAY[level])
        offset = blocks // 2 - 2 * members

        def body(mask, received_ref, rhs_ref, matrix, *outs):
            sent = outs[0]
            chunks = summed_chunks(received_ref, order)
            if not known:
                write_solution(outs[1], own_chunk(chunks, lax.axis_index(FRONT)))
            out, shift = products(packing.unpack(chunks), matrix, offset * rows_dev, members * rows_dev)
            own = lax.axis_index(LEAF) % members
            gates = mask[...].astype(jnp.float32)
            right = both_parts(rhs_ref, level - 1)
            for a in range(members):
                lane = shift + a * rows_dev
                part = out[:, lane : lane + rows_dev] * gates[:, offset + a : offset + a + 1]
                strips = packing.pack(jnp.where(own == a, right, 0.0) - part)
                put(sent, range(a * copies, (a + 1) * copies), strips)

        outs = (sent_shape(members * copies),) + (() if known else (sol_shape,))
        return call(body, outs, (tile_mask, received, rhs, upd_blocks))

    def combine(level, received, solution):
        members = blocks >> (level + 1)
        kept = copies_of(WAY[level])
        copies = fronts if WAY[level] == THEN_FRONT else 1

        def body(received_ref, sent, *outs):
            chunks = summed_chunks(received_ref, [[m * kept + k for m in range(members)] for k in range(kept)])
            if solution:
                own = lax.axis_index("x") if kept > 1 else 0
                write_solution(outs[0], own_chunk(chunks, own))
            for k in range(kept):
                put(sent, range(k * copies, (k + 1) * copies), chunks[k])

        outs = (sent_shape(kept * copies),) + ((sol_shape,) if solution else ())
        return call(body, outs, (received,))

    def exchange(level, sent, solution):
        members = blocks >> (level + 1)
        group = LEAF[len(LEAF) - (levels - level) :]
        if WAY[level] == WITH_FRONT:
            return over(sent, group + FRONT), by_front(members), None
        if WAY[level] == THEN_FRONT:
            sent, *solved = combine(level, over(sent, group), solution)
            return over(sent, FRONT), by_front(1), solved[0] if solution else None
        sent, *solved = combine(level, over(sent, group + FRONT[:1]), solution)
        both = lax.all_gather(sent, FRONT[1], axis=0, tiled=True)
        order = [[(c % axes["core"]) * axes["x"] + c // axes["core"]] for c in range(fronts)]
        return both, order, solved[0] if solution else None

    def finish(received, solved):
        def body(received_ref, *refs):
            out = refs[-1]
            write_solution(out.at[0], summed_chunks(received_ref, [range(received.shape[0])])[0])
            for level in range(1, levels):
                out[level] = refs[level - 1][...]

        return call(body, same(rhs), (received, *solved))

    received, order = over(sent, FRONT), by_front(1)
    solved = [None] * levels
    for level in range(levels - 1, 0, -1):
        received, order, solved[level] = exchange(level, invert(level, received, order), True)
        sent, *rest = update(level, received, order, solved[level] is not None)
        if rest:
            solved[level] = rest[0]
        received, order, _ = exchange(level, sent, False)
    return finish(over(invert(0, received, order), LEAF[1:]), solved[1:])


def solution(mesh):
    finer = Mesh(mesh.devices.reshape(2, 2, 2, 2, 2, 2, 4, 2), LEAF + FRONT)
    placed = (
        P(None, None, None, LEAF + FRONT),
        P(None, LEAF, FRONT),
        P(None, LEAF, FRONT),
        P(LEAF, None),
    )
    return jax.shard_map(
        shards,
        mesh=finer,
        in_specs=placed,
        out_specs=P(None, None, None, LEAF + FRONT),
        check_vma=False,
    )
```

```python
import jax
import jax.numpy as jnp
from jax import lax
from jax.experimental import pallas as pl
from jax.experimental.pallas import tpu as pltpu
from jax.sharding import Mesh
from jax.sharding import PartitionSpec as P

LEAF = ("y1", "y0", "z3", "z2", "z1", "z0")
FRONT = ("x", "core")
WITH_FRONT, THEN_FRONT, WITH_X_THEN_CORE = range(3)
WAY = {4: WITH_FRONT, 3: WITH_FRONT, 2: WITH_X_THEN_CORE, 1: THEN_FRONT}
STRIP = 4


def lane_window(columns, start, width):
    first = start // 128 * 128
    last = min(-(-(start + width) // 128) * 128, columns)
    return first, last


def whole(space=pltpu.VMEM):
    return pl.BlockSpec(memory_space=space)


def call(body, outs, inputs, space=pltpu.VMEM, scratch=(), cost=None):
    return pl.pallas_call(
        body,
        out_shape=outs,
        in_specs=[whole(space)] * len(inputs),
        out_specs=jax.tree.map(lambda _: whole(), outs),
        scratch_shapes=scratch,
        cost_estimate=cost,
        compiler_params=pltpu.CompilerParams(vmem_limit_bytes=16 * 2**20),
    )(*inputs)


class Packing:
    def __init__(self, rows, lanes):
        self.rows, self.lanes = rows, lanes
        self.groups = 128 // lanes
        self.strips = -(-rows // (self.groups * STRIP))
        self.shape = (self.strips, STRIP, self.groups * lanes)

    def first_row(self, group, strip):
        return (group * self.strips + strip) * STRIP

    def pack(self, block):
        strips = []
        for j in range(self.strips):
            pieces = []
            for g in range(self.groups):
                row = self.first_row(g, j)
                if row < self.rows:
                    pieces.append(block[row : row + STRIP])
                else:
                    pieces.append(jnp.zeros((STRIP, self.lanes), jnp.float32))
            strips.append(jnp.concatenate(pieces, axis=1))
        return strips

    def unpack(self, chunks):
        rows = []
        for g in range(self.groups):
            for j in range(self.strips):
                if self.first_row(g, j) < self.rows:
                    low = g * self.lanes
                    rows.append(jnp.concatenate([c[j][:, low : low + self.lanes] for c in chunks], axis=1))
        return jnp.concatenate(rows, axis=0)


def summed_chunks(received, order):
    chunks = []
    for messages in order:
        strips = []
        for j in range(received.shape[1]):
            total = received[messages[0], j].astype(jnp.float32)
            for m in messages[1:]:
                total = total + received[m, j].astype(jnp.float32)
            strips.append(total)
        chunks.append(strips)
    return chunks


def own_chunk(chunks, own):
    strips = []
    for j in range(len(chunks[0])):
        total = jnp.zeros(chunks[0][j].shape, jnp.float32)
        for c in range(len(chunks)):
            total = total + jnp.where(own == c, chunks[c][j], 0.0)
        strips.append(total)
    return strips


def products(block, matrix, start, width):
    half = block.shape[0] // 2
    real, imag = block[:half], block[half:]
    upper = jnp.concatenate([real, -imag], axis=1)
    lower = jnp.concatenate([imag, real], axis=1)
    stacked = jnp.concatenate([upper, lower], axis=0).astype(jnp.bfloat16)
    first, last = lane_window(matrix.shape[2], start, width)
    weights = matrix[:, :, first:last].reshape(-1, last - first)
    return jnp.dot(stacked, weights, preferred_element_type=jnp.float32), start - first


def put(sent, slots, strips):
    for j, strip in enumerate(strips):
        value = strip.astype(jnp.bfloat16)
        for slot in slots:
            sent[slot, j] = value


def shards(rhs, inv_blocks, upd_blocks, tile_mask):
    axes = {name: lax.axis_size(name) for name in LEAF + FRONT}
    fronts = axes["x"] * axes["core"]
    blocks = 1
    for name in LEAF:
        blocks *= axes[name]
    levels, _, rhs_count, rows_dev = rhs.shape
    packing = Packing(2 * rhs_count, rows_dev)

    def sent_shape(count):
        return jax.ShapeDtypeStruct((count,) + packing.shape, jnp.bfloat16)

    sol_shape = jax.ShapeDtypeStruct((2, rhs_count, rows_dev), jnp.float32)

    def both_parts(rhs_ref, level):
        return jnp.concatenate([rhs_ref[level, 0], rhs_ref[level, 1]], axis=0)

    def write_solution(sol, strips):
        value = packing.unpack([strips])
        sol[0] = value[:rhs_count]
        sol[1] = value[rhs_count:]

    def over(value, names):
        return lax.all_to_all(value, names, 0, 0, tiled=True)

    def by_front(count):
        return [[m * fronts + c for m in range(count)] for c in range(fronts)]

    def copies_of(way):
        return {WITH_FRONT: fronts, WITH_X_THEN_CORE: axes["x"], THEN_FRONT: 1}[way]

    def first_body(rhs_hbm, sent, rhs_ref, sem):
        move = pltpu.make_async_copy(rhs_hbm, rhs_ref, sem)
        move.start()
        move.wait()
        put(sent, range(fronts), packing.pack(both_parts(rhs_ref, levels - 1)))

    def same(array):
        return jax.ShapeDtypeStruct(array.shape, array.dtype)

    sent, rhs = call(
        first_body,
        (sent_shape(fronts), same(rhs)),
        (pltpu.with_memory_space_constraint(rhs, pltpu.HBM),),
        pltpu.HBM,
        (pltpu.SemaphoreType.DMA(()),),
        pl.CostEstimate(flops=10**10, transcendentals=0, bytes_accessed=2 * 10**7),
    )

    def invert(level, received, order):
        members = blocks >> (level + 1)
        copies = copies_of(WAY[level]) if level > 0 else 1

        def body(received_ref, matrix, sent):
            block = packing.unpack(summed_chunks(received_ref, order))
            out, shift = products(block, matrix, (blocks - 2 * members) * rows_dev, members * rows_dev)
            for a in range(members):
                lane = shift + a * rows_dev
                strips = packing.pack(out[:, lane : lane + rows_dev])
                put(sent, range(a * copies, (a + 1) * copies), strips)

        return call(body, sent_shape(members * copies), (received, inv_blocks))

    def update(level, received, order, known):
        members = blocks >> (level + 1)
        copies = copies_of(WAY[level])
        offset = blocks // 2 - 2 * members

        def body(mask, received_ref, rhs_ref, matrix, *outs):
            sent = outs[0]
            chunks = summed_chunks(received_ref, order)
            if not known:
                write_solution(outs[1], own_chunk(chunks, lax.axis_index(FRONT)))
            out, shift = products(packing.unpack(chunks), matrix, offset * rows_dev, members * rows_dev)
            own = lax.axis_index(LEAF) % members
            gates = mask[...].astype(jnp.float32)
            right = both_parts(rhs_ref, level - 1)
            for a in range(members):
                lane = shift + a * rows_dev
                part = out[:, lane : lane + rows_dev] * gates[:, offset + a : offset + a + 1]
                strips = packing.pack(jnp.where(own == a, right, 0.0) - part)
                put(sent, range(a * copies, (a + 1) * copies), strips)

        outs = (sent_shape(members * copies),) + (() if known else (sol_shape,))
        return call(body, outs, (tile_mask, received, rhs, upd_blocks))

    def combine(level, received, solution):
        members = blocks >> (level + 1)
        kept = copies_of(WAY[level])
        copies = fronts if WAY[level] == THEN_FRONT else 1

        def body(received_ref, sent, *outs):
            chunks = summed_chunks(received_ref, [[m * kept + k for m in range(members)] for k in range(kept)])
            if solution:
                own = lax.axis_index("x") if kept > 1 else 0
                write_solution(outs[0], own_chunk(chunks, own))
            for k in range(kept):
                put(sent, range(k * copies, (k + 1) * copies), chunks[k])

        outs = (sent_shape(kept * copies),) + ((sol_shape,) if solution else ())
        return call(body, outs, (received,))

    def exchange(level, sent, solution):
        members = blocks >> (level + 1)
        group = LEAF[len(LEAF) - (levels - level) :]
        if WAY[level] == WITH_FRONT:
            return over(sent, group + FRONT), by_front(members), None
        if WAY[level] == THEN_FRONT:
            sent, *solved = combine(level, over(sent, group), solution)
            return over(sent, FRONT), by_front(1), solved[0] if solution else None
        sent, *solved = combine(level, over(sent, group + FRONT[:1]), solution)
        both = lax.all_gather(sent, FRONT[1], axis=0, tiled=True)
        order = [[(c % axes["core"]) * axes["x"] + c // axes["core"]] for c in range(fronts)]
        return both, order, solved[0] if solution else None

    def finish(received, solved):
        def body(received_ref, *refs):
            out = refs[-1]
            write_solution(out.at[0], summed_chunks(received_ref, [range(received.shape[0])])[0])
            for level in range(1, levels):
                out[level] = refs[level - 1][...]

        return call(body, same(rhs), (received, *solved))

    received, order = over(sent, FRONT), by_front(1)
    solved = [None] * levels
    for level in range(levels - 1, 0, -1):
        received, order, solved[level] = exchange(level, invert(level, received, order), True)
        sent, *rest = update(level, received, order, solved[level] is not None)
        if rest:
            solved[level] = rest[0]
        received, order, _ = exchange(level, sent, False)
    return finish(over(invert(0, received, order), LEAF[1:]), solved[1:])


def solution(mesh):
    finer = Mesh(mesh.devices.reshape(2, 2, 2, 2, 2, 2, 4, 2), LEAF + FRONT)
    placed = (
        P(None, None, None, LEAF + FRONT),
        P(None, LEAF, FRONT),
        P(None, LEAF, FRONT),
        P(LEAF, None),
    )
    return jax.shard_map(
        shards,
        mesh=finer,
        in_specs=placed,
        out_specs=P(None, None, None, LEAF + FRONT),
        check_vma=False,
    )
```

```python
import jax
import jax.numpy as jnp
from jax import lax
from jax.experimental import pallas as pl
from jax.experimental.pallas import tpu as pltpu
from jax.sharding import Mesh
from jax.sharding import PartitionSpec as P

LEAF = ("y1", "y0", "z3", "z2", "z1", "z0")
FRONT = ("x", "core")
WITH_FRONT, THEN_FRONT, WITH_X_THEN_CORE = range(3)
WAY = {4: WITH_FRONT, 3: WITH_FRONT, 2: WITH_X_THEN_CORE, 1: THEN_FRONT}
GROUP = {
    4: ("z0", "x", "core"),
    3: ("z0", "x", "core", "z1"),
    2: ("z0", "x", "z1", "z2"),
    1: ("z1", "z2", "z3", "z0"),
    0: ("z3", "z2", "z1", "z0", "y0"),
}
STRIP = 4


def lane_window(columns, start, width):
    first = start // 128 * 128
    last = min(-(-(start + width) // 128) * 128, columns)
    return first, last


def whole(space=pltpu.VMEM):
    return pl.BlockSpec(memory_space=space)


def call(body, outs, inputs, space=pltpu.VMEM, scratch=(), cost=None):
    return pl.pallas_call(
        body,
        out_shape=outs,
        in_specs=[whole(space)] * len(inputs),
        out_specs=jax.tree.map(lambda _: whole(), outs),
        scratch_shapes=scratch,
        cost_estimate=cost,
        compiler_params=pltpu.CompilerParams(vmem_limit_bytes=16 * 2**20),
    )(*inputs)


class Packing:
    def __init__(self, rows, lanes):
        self.rows, self.lanes = rows, lanes
        self.groups = 128 // lanes
        self.strips = -(-rows // (self.groups * STRIP))
        self.shape = (self.strips, STRIP, self.groups * lanes)

    def first_row(self, group, strip):
        return (group * self.strips + strip) * STRIP

    def pack(self, block):
        strips = []
        for j in range(self.strips):
            pieces = []
            for g in range(self.groups):
                row = self.first_row(g, j)
                if row < self.rows:
                    pieces.append(block[row : row + STRIP])
                else:
                    pieces.append(jnp.zeros((STRIP, self.lanes), jnp.float32))
            strips.append(jnp.concatenate(pieces, axis=1))
        return strips

    def unpack(self, chunks):
        rows = []
        for g in range(self.groups):
            for j in range(self.strips):
                if self.first_row(g, j) < self.rows:
                    low = g * self.lanes
                    rows.append(jnp.concatenate([c[j][:, low : low + self.lanes] for c in chunks], axis=1))
        return jnp.concatenate(rows, axis=0)


def summed_chunks(received, order):
    chunks = []
    for messages in order:
        strips = []
        for j in range(received.shape[1]):
            total = received[messages[0], j].astype(jnp.float32)
            for m in messages[1:]:
                total = total + received[m, j].astype(jnp.float32)
            strips.append(total)
        chunks.append(strips)
    return chunks


def own_chunk(chunks, own):
    strips = []
    for j in range(len(chunks[0])):
        total = jnp.zeros(chunks[0][j].shape, jnp.float32)
        for c in range(len(chunks)):
            total = total + jnp.where(own == c, chunks[c][j], 0.0)
        strips.append(total)
    return strips


def products(block, matrix, start, width):
    half = block.shape[0] // 2
    real, imag = block[:half], block[half:]
    upper = jnp.concatenate([real, -imag], axis=1)
    lower = jnp.concatenate([imag, real], axis=1)
    stacked = jnp.concatenate([upper, lower], axis=0).astype(jnp.bfloat16)
    first, last = lane_window(matrix.shape[2], start, width)
    weights = matrix[:, :, first:last].reshape(-1, last - first)
    return jnp.dot(stacked, weights, preferred_element_type=jnp.float32), start - first


def put(sent, slots, strips):
    for j, strip in enumerate(strips):
        value = strip.astype(jnp.bfloat16)
        for slot in slots:
            sent[slot, j] = value


def shards(rhs, inv_blocks, upd_blocks, tile_mask):
    axes = {name: lax.axis_size(name) for name in LEAF + FRONT}
    fronts = axes["x"] * axes["core"]
    blocks = 1
    for name in LEAF:
        blocks *= axes[name]
    levels, _, rhs_count, rows_dev = rhs.shape
    packing = Packing(2 * rhs_count, rows_dev)

    def sent_shape(count):
        return jax.ShapeDtypeStruct((count,) + packing.shape, jnp.bfloat16)

    sol_shape = jax.ShapeDtypeStruct((2, rhs_count, rows_dev), jnp.float32)

    def both_parts(rhs_ref, level):
        return jnp.concatenate([rhs_ref[level, 0], rhs_ref[level, 1]], axis=0)

    def write_solution(sol, strips):
        value = packing.unpack([strips])
        sol[0] = value[:rhs_count]
        sol[1] = value[rhs_count:]

    def over(value, names):
        return lax.all_to_all(value, names, 0, 0, tiled=True)

    def slot(names, member, x=0, core=0):
        place = 0
        for name in names:
            if name in FRONT:
                here = x if name == "x" else core
            else:
                here = member >> LEAF[::-1].index(name) & 1
            place = place * axes[name] + here
        return place

    def by_front(names, count):
        pairs = [(x, core) for x in range(axes["x"]) for core in range(axes["core"])]
        return [[slot(names, m, *pair) for m in range(count)] for pair in pairs]

    def member_slots(level, member):
        names = GROUP[level]
        xs = range(axes["x"] if "x" in names else 1)
        cores = range(axes["core"] if "core" in names else 1)
        return [slot(names, member, x, core) for x in xs for core in cores]

    def message_count(level):
        return len(member_slots(level, 0)) * (blocks >> (level + 1))

    def first_body(rhs_hbm, sent, rhs_ref, sem):
        move = pltpu.make_async_copy(rhs_hbm, rhs_ref, sem)
        move.start()
        move.wait()
        put(sent, range(fronts), packing.pack(both_parts(rhs_ref, levels - 1)))

    def same(array):
        return jax.ShapeDtypeStruct(array.shape, array.dtype)

    sent, rhs = call(
        first_body,
        (sent_shape(fronts), same(rhs)),
        (pltpu.with_memory_space_constraint(rhs, pltpu.HBM),),
        pltpu.HBM,
        (pltpu.SemaphoreType.DMA(()),),
        pl.CostEstimate(flops=10**10, transcendentals=0, bytes_accessed=2 * 10**7),
    )

    def invert(level, received, order):
        members = blocks >> (level + 1)

        def body(received_ref, matrix, sent):
            block = packing.unpack(summed_chunks(received_ref, order))
            out, shift = products(block, matrix, (blocks - 2 * members) * rows_dev, members * rows_dev)
            for a in range(members):
                lane = shift + a * rows_dev
                strips = packing.pack(out[:, lane : lane + rows_dev])
                put(sent, member_slots(level, a), strips)

        return call(body, sent_shape(message_count(level)), (received, inv_blocks))

    def update(level, received, order, known):
        members = blocks >> (level + 1)
        offset = blocks // 2 - 2 * members

        def body(mask, received_ref, rhs_ref, matrix, *outs):
            sent = outs[0]
            chunks = summed_chunks(received_ref, order)
            if not known:
                write_solution(outs[1], own_chunk(chunks, lax.axis_index(FRONT)))
            out, shift = products(packing.unpack(chunks), matrix, offset * rows_dev, members * rows_dev)
            own = lax.axis_index(LEAF) % members
            gates = mask[...].astype(jnp.float32)
            right = both_parts(rhs_ref, level - 1)
            for a in range(members):
                lane = shift + a * rows_dev
                part = out[:, lane : lane + rows_dev] * gates[:, offset + a : offset + a + 1]
                strips = packing.pack(jnp.where(own == a, right, 0.0) - part)
                put(sent, member_slots(level, a), strips)

        outs = (sent_shape(message_count(level)),) + (() if known else (sol_shape,))
        return call(body, outs, (tile_mask, received, rhs, upd_blocks))

    def combine(level, received, solution):
        members = blocks >> (level + 1)
        kept = axes["x"] if "x" in GROUP[level] else 1
        copies = fronts if WAY[level] == THEN_FRONT else 1

        def body(received_ref, sent, *outs):
            chunks = summed_chunks(received_ref, [[slot(GROUP[level], m, k) for m in range(members)] for k in range(kept)])
            if solution:
                own = lax.axis_index("x") if kept > 1 else 0
                write_solution(outs[0], own_chunk(chunks, own))
            for k in range(kept):
                put(sent, range(k * copies, (k + 1) * copies), chunks[k])

        outs = (sent_shape(kept * copies),) + ((sol_shape,) if solution else ())
        return call(body, outs, (received,))

    def exchange(level, sent, solution):
        names = GROUP[level]
        if WAY[level] == WITH_FRONT:
            return over(sent, names), by_front(names, blocks >> (level + 1)), None
        sent, *solved = combine(level, over(sent, names), solution)
        if WAY[level] == THEN_FRONT:
            return over(sent, FRONT), by_front(FRONT, 1), solved[0] if solution else None
        both = lax.all_gather(sent, "core", axis=0, tiled=True)
        return both, by_front(("core", "x"), 1), solved[0] if solution else None

    def finish(received, solved):
        def body(received_ref, *refs):
            out = refs[-1]
            write_solution(out.at[0], summed_chunks(received_ref, [range(received.shape[0])])[0])
            for level in range(1, levels):
                out[level] = refs[level - 1][...]

        return call(body, same(rhs), (received, *solved))

    received, order = over(sent, FRONT), by_front(FRONT, 1)
    solved = [None] * levels
    for level in range(levels - 1, 0, -1):
        received, order, solved[level] = exchange(level, invert(level, received, order), True)
        sent, *rest = update(level, received, order, solved[level] is not None)
        if rest:
            solved[level] = rest[0]
        received, order, _ = exchange(level, sent, False)
    return finish(over(invert(0, received, order), GROUP[0]), solved[1:])


def solution(mesh):
    finer = Mesh(mesh.devices.reshape(2, 2, 2, 2, 2, 2, 4, 2), LEAF + FRONT)
    placed = (
        P(None, None, None, LEAF + FRONT),
        P(None, LEAF, FRONT),
        P(None, LEAF, FRONT),
        P(LEAF, None),
    )
    return jax.shard_map(
        shards,
        mesh=finer,
        in_specs=placed,
        out_specs=P(None, None, None, LEAF + FRONT),
        check_vma=False,
    )
```

```python
import jax
import jax.numpy as jnp
from jax import lax
from jax.experimental import pallas as pl
from jax.experimental.pallas import tpu as pltpu
from jax.sharding import Mesh
from jax.sharding import PartitionSpec as P

LEAF = ("y1", "y0", "z3", "z2", "z1", "z0")
FRONT = ("x", "core")
WITH_FRONT, THEN_FRONT, WITH_X_THEN_CORE = range(3)
WAY = {4: WITH_FRONT, 3: WITH_FRONT, 2: WITH_X_THEN_CORE, 1: WITH_X_THEN_CORE}
GROUP = {
    4: ("z0", "x", "core"),
    3: ("z0", "x", "core", "z1"),
    2: ("z0", "x", "z1", "z2"),
    1: ("z0", "z1", "z2", "z3", "x"),
    0: ("z3", "z2", "z1", "z0", "y0"),
}
STRIP = 2


def lane_window(columns, start, width):
    first = start // 128 * 128
    last = min(-(-(start + width) // 128) * 128, columns)
    return first, last


def whole(space=pltpu.VMEM):
    return pl.BlockSpec(memory_space=space)


def call(body, outs, inputs, space=pltpu.VMEM, scratch=(), cost=None):
    return pl.pallas_call(
        body,
        out_shape=outs,
        in_specs=[whole(space)] * len(inputs),
        out_specs=jax.tree.map(lambda _: whole(), outs),
        scratch_shapes=scratch,
        cost_estimate=cost,
        compiler_params=pltpu.CompilerParams(vmem_limit_bytes=16 * 2**20),
    )(*inputs)


class Packing:
    def __init__(self, rows, lanes):
        self.lanes = lanes
        self.depth = rows * lanes // 128
        self.groups = 128 // lanes
        self.left = 128 - self.groups * lanes
        self.rest = rows - self.groups * self.depth
        self.units = lanes // self.left
        assert rows * lanes == self.depth * 128 and self.rest * self.units == self.depth
        self.shape = (self.depth // STRIP, STRIP, 128)

    def pack(self, block):
        top = self.groups * self.depth
        pieces = [block[g * self.depth : (g + 1) * self.depth] for g in range(self.groups)]
        tail = [block[top:, u * self.left : (u + 1) * self.left] for u in range(self.units)]
        packed = jnp.concatenate([*pieces, jnp.concatenate(tail, axis=0)], axis=1)
        packed = packed.astype(jnp.bfloat16)
        return [packed[k : k + STRIP] for k in range(0, self.depth, STRIP)]

    def unpack(self, chunks):
        full = [jnp.concatenate(strips, axis=0) for strips in chunks]
        rows = []
        for g in range(self.groups):
            low = g * self.lanes
            rows.append(jnp.concatenate([f[:, low : low + self.lanes] for f in full], axis=1))
        low = self.groups * self.lanes
        tail = [f[u * self.rest : (u + 1) * self.rest, low:] for f in full for u in range(self.units)]
        return jnp.concatenate([*rows, jnp.concatenate(tail, axis=1)], axis=0)


def summed_chunks(received, order):
    chunks = []
    for messages in order:
        strips = []
        for j in range(received.shape[1]):
            total = received[messages[0], j].astype(jnp.float32)
            for m in messages[1:]:
                total = total + received[m, j].astype(jnp.float32)
            strips.append(total)
        chunks.append(strips)
    return chunks


def own_chunk(chunks, own):
    strips = []
    for j in range(len(chunks[0])):
        total = jnp.zeros(chunks[0][j].shape, jnp.float32)
        for c in range(len(chunks)):
            total = total + jnp.where(own == c, chunks[c][j], 0.0)
        strips.append(total)
    return strips


def products(block, matrix, start, width):
    half = block.shape[0] // 2
    real, imag = block[:half], block[half:]
    upper = jnp.concatenate([real, -imag], axis=1)
    lower = jnp.concatenate([imag, real], axis=1)
    stacked = jnp.concatenate([upper, lower], axis=0).astype(jnp.bfloat16)
    first, last = lane_window(matrix.shape[2], start, width)
    weights = matrix[:, :, first:last].reshape(-1, last - first)
    return jnp.dot(stacked, weights, preferred_element_type=jnp.float32), start - first


def put(sent, slots, strips):
    for j, strip in enumerate(strips):
        value = strip.astype(jnp.bfloat16)
        for slot in slots:
            sent[slot, j] = value


def shards(rhs, inv_blocks, upd_blocks, tile_mask):
    axes = {name: lax.axis_size(name) for name in LEAF + FRONT}
    fronts = axes["x"] * axes["core"]
    blocks = 1
    for name in LEAF:
        blocks *= axes[name]
    levels, _, rhs_count, rows_dev = rhs.shape
    packing = Packing(2 * rhs_count, rows_dev)

    def sent_shape(count):
        return jax.ShapeDtypeStruct((count,) + packing.shape, jnp.bfloat16)

    sol_shape = jax.ShapeDtypeStruct((2, rhs_count, rows_dev), jnp.float32)

    def both_parts(rhs_ref, level):
        return jnp.concatenate([rhs_ref[level, 0], rhs_ref[level, 1]], axis=0)

    def write_solution(sol, strips):
        value = packing.unpack([strips])
        sol[0] = value[:rhs_count]
        sol[1] = value[rhs_count:]

    def over(value, names):
        return lax.all_to_all(value, names, 0, 0, tiled=True)

    def slot(names, member, x=0, core=0):
        place = 0
        for name in names:
            if name in FRONT:
                here = x if name == "x" else core
            else:
                here = member >> LEAF[::-1].index(name) & 1
            place = place * axes[name] + here
        return place

    def by_front(names, count):
        pairs = [(x, core) for x in range(axes["x"]) for core in range(axes["core"])]
        return [[slot(names, m, *pair) for m in range(count)] for pair in pairs]

    def member_slots(level, member):
        names = GROUP[level]
        xs = range(axes["x"] if "x" in names else 1)
        cores = range(axes["core"] if "core" in names else 1)
        return [slot(names, member, x, core) for x in xs for core in cores]

    def message_count(level):
        return len(member_slots(level, 0)) * (blocks >> (level + 1))

    def first_body(rhs_hbm, sent, rhs_ref, sem):
        move = pltpu.make_async_copy(rhs_hbm, rhs_ref, sem)
        move.start()
        move.wait()
        put(sent, range(fronts), packing.pack(both_parts(rhs_ref, levels - 1)))

    def same(array):
        return jax.ShapeDtypeStruct(array.shape, array.dtype)

    sent, rhs = call(
        first_body,
        (sent_shape(fronts), same(rhs)),
        (pltpu.with_memory_space_constraint(rhs, pltpu.HBM),),
        pltpu.HBM,
        (pltpu.SemaphoreType.DMA(()),),
        pl.CostEstimate(flops=10**10, transcendentals=0, bytes_accessed=2 * 10**7),
    )

    def invert(level, received, order):
        members = blocks >> (level + 1)

        def body(received_ref, matrix, sent):
            block = packing.unpack(summed_chunks(received_ref, order))
            out, shift = products(block, matrix, (blocks - 2 * members) * rows_dev, members * rows_dev)
            for a in range(members):
                lane = shift + a * rows_dev
                strips = packing.pack(out[:, lane : lane + rows_dev])
                put(sent, member_slots(level, a), strips)

        return call(body, sent_shape(message_count(level)), (received, inv_blocks))

    def update(level, received, order, known):
        members = blocks >> (level + 1)
        offset = blocks // 2 - 2 * members

        def body(mask, received_ref, rhs_ref, matrix, *outs):
            sent = outs[0]
            chunks = summed_chunks(received_ref, order)
            if not known:
                write_solution(outs[1], own_chunk(chunks, lax.axis_index(FRONT)))
            out, shift = products(packing.unpack(chunks), matrix, offset * rows_dev, members * rows_dev)
            own = lax.axis_index(LEAF) % members
            gates = mask[...].astype(jnp.float32)
            right = both_parts(rhs_ref, level - 1)
            for a in range(members):
                lane = shift + a * rows_dev
                part = out[:, lane : lane + rows_dev] * gates[:, offset + a : offset + a + 1]
                strips = packing.pack(jnp.where(own == a, right, 0.0) - part)
                put(sent, member_slots(level, a), strips)

        outs = (sent_shape(message_count(level)),) + (() if known else (sol_shape,))
        return call(body, outs, (tile_mask, received, rhs, upd_blocks))

    def combine(level, received, solution):
        members = blocks >> (level + 1)
        kept = axes["x"] if "x" in GROUP[level] else 1
        copies = fronts if WAY[level] == THEN_FRONT else 1

        def body(received_ref, sent, *outs):
            chunks = summed_chunks(received_ref, [[slot(GROUP[level], m, k) for m in range(members)] for k in range(kept)])
            if solution:
                own = lax.axis_index("x") if kept > 1 else 0
                write_solution(outs[0], own_chunk(chunks, own))
            for k in range(kept):
                put(sent, range(k * copies, (k + 1) * copies), chunks[k])

        outs = (sent_shape(kept * copies),) + ((sol_shape,) if solution else ())
        return call(body, outs, (received,))

    def exchange(level, sent, solution):
        names = GROUP[level]
        if WAY[level] == WITH_FRONT:
            return over(sent, names), by_front(names, blocks >> (level + 1)), None
        sent, *solved = combine(level, over(sent, names), solution)
        if WAY[level] == THEN_FRONT:
            return over(sent, FRONT), by_front(FRONT, 1), solved[0] if solution else None
        both = lax.all_gather(sent, "core", axis=0, tiled=True)
        return both, by_front(("core", "x"), 1), solved[0] if solution else None

    def finish(received, solved):
        def body(received_ref, *refs):
            out = refs[-1]
            write_solution(out.at[0], summed_chunks(received_ref, [range(received.shape[0])])[0])
            for level in range(1, levels):
                out[level] = refs[level - 1][...]

        return call(body, same(rhs), (received, *solved))

    received, order = over(sent, FRONT), by_front(FRONT, 1)
    solved = [None] * levels
    for level in range(levels - 1, 0, -1):
        received, order, solved[level] = exchange(level, invert(level, received, order), True)
        sent, *rest = update(level, received, order, solved[level] is not None)
        if rest:
            solved[level] = rest[0]
        received, order, _ = exchange(level, sent, False)
    return finish(over(invert(0, received, order), GROUP[0]), solved[1:])


def solution(mesh):
    finer = Mesh(mesh.devices.reshape(2, 2, 2, 2, 2, 2, 4, 2), LEAF + FRONT)
    placed = (
        P(None, None, None, LEAF + FRONT),
        P(None, LEAF, FRONT),
        P(None, LEAF, FRONT),
        P(LEAF, None),
    )
    return jax.shard_map(
        shards,
        mesh=finer,
        in_specs=placed,
        out_specs=P(None, None, None, LEAF + FRONT),
        check_vma=False,
    )
```

```python
import jax
import jax.numpy as jnp
from jax import lax
from jax.experimental import pallas as pl
from jax.experimental.pallas import tpu as pltpu
from jax.sharding import Mesh
from jax.sharding import PartitionSpec as P

LEAF = ("y1", "y0", "z3", "z2", "z1", "z0")
FRONT = ("x", "core")
WITH_FRONT, THEN_FRONT, WITH_X_THEN_CORE = range(3)
WAY = {4: WITH_FRONT, 3: WITH_FRONT, 2: WITH_X_THEN_CORE, 1: THEN_FRONT}
GROUP = {
    4: ("z0", "x", "core"),
    3: ("z0", "x", "core", "z1"),
    2: ("z0", "x", "z1", "z2"),
    1: ("z1", "z2", "z3", "z0"),
    0: ("z3", "z2", "z1", "z0", "y0"),
}
WIRE = {4: jnp.float32, 3: jnp.float32, 2: jnp.bfloat16, 1: jnp.bfloat16, 0: jnp.bfloat16}
STRIP = 4


def lane_window(columns, start, width):
    first = start // 128 * 128
    last = min(-(-(start + width) // 128) * 128, columns)
    return first, last


def whole(space=pltpu.VMEM):
    return pl.BlockSpec(memory_space=space)


def call(body, outs, inputs, space=pltpu.VMEM, scratch=(), cost=None):
    return pl.pallas_call(
        body,
        out_shape=outs,
        in_specs=[whole(space)] * len(inputs),
        out_specs=jax.tree.map(lambda _: whole(), outs),
        scratch_shapes=scratch,
        cost_estimate=cost,
        compiler_params=pltpu.CompilerParams(vmem_limit_bytes=16 * 2**20),
    )(*inputs)


class Packing:
    def __init__(self, rows, lanes):
        self.rows, self.lanes = rows, lanes
        self.groups = 128 // lanes
        self.strips = -(-rows // (self.groups * STRIP))
        self.shape = (self.strips, STRIP, self.groups * lanes)

    def first_row(self, group, strip):
        return (group * self.strips + strip) * STRIP

    def pack(self, block):
        strips = []
        for j in range(self.strips):
            pieces = []
            for g in range(self.groups):
                row = self.first_row(g, j)
                if row < self.rows:
                    pieces.append(block[row : row + STRIP])
                else:
                    pieces.append(jnp.zeros((STRIP, self.lanes), jnp.float32))
            strips.append(jnp.concatenate(pieces, axis=1))
        return strips

    def unpack(self, chunks):
        rows = []
        for g in range(self.groups):
            for j in range(self.strips):
                if self.first_row(g, j) < self.rows:
                    low = g * self.lanes
                    rows.append(jnp.concatenate([c[j][:, low : low + self.lanes] for c in chunks], axis=1))
        return jnp.concatenate(rows, axis=0)


def summed_chunks(received, order):
    chunks = []
    for messages in order:
        strips = []
        for j in range(received.shape[1]):
            total = received[messages[0], j].astype(jnp.float32)
            for m in messages[1:]:
                total = total + received[m, j].astype(jnp.float32)
            strips.append(total)
        chunks.append(strips)
    return chunks


def own_chunk(chunks, own):
    strips = []
    for j in range(len(chunks[0])):
        total = jnp.zeros(chunks[0][j].shape, jnp.float32)
        for c in range(len(chunks)):
            total = total + jnp.where(own == c, chunks[c][j], 0.0)
        strips.append(total)
    return strips


def products(block, matrix, start, width):
    half = block.shape[0] // 2
    real, imag = block[:half], block[half:]
    upper = jnp.concatenate([real, -imag], axis=1)
    lower = jnp.concatenate([imag, real], axis=1)
    stacked = jnp.concatenate([upper, lower], axis=0).astype(jnp.bfloat16)
    first, last = lane_window(matrix.shape[2], start, width)
    weights = matrix[:, :, first:last].reshape(-1, last - first)
    return jnp.dot(stacked, weights, preferred_element_type=jnp.float32), start - first


def put(sent, slots, strips):
    for j, strip in enumerate(strips):
        value = strip.astype(sent.dtype)
        for slot in slots:
            sent[slot, j] = value


def shards(rhs, inv_blocks, upd_blocks, tile_mask):
    axes = {name: lax.axis_size(name) for name in LEAF + FRONT}
    fronts = axes["x"] * axes["core"]
    blocks = 1
    for name in LEAF:
        blocks *= axes[name]
    levels, _, rhs_count, rows_dev = rhs.shape
    packing = Packing(2 * rhs_count, rows_dev)

    def sent_shape(count, dtype=jnp.bfloat16):
        return jax.ShapeDtypeStruct((count,) + packing.shape, dtype)

    sol_shape = jax.ShapeDtypeStruct((2, rhs_count, rows_dev), jnp.float32)

    def both_parts(rhs_ref, level):
        return jnp.concatenate([rhs_ref[level, 0], rhs_ref[level, 1]], axis=0)

    def write_solution(sol, strips):
        value = packing.unpack([strips])
        sol[0] = value[:rhs_count]
        sol[1] = value[rhs_count:]

    def over(value, names):
        return lax.all_to_all(value, names, 0, 0, tiled=True)

    def slot(names, member, x=0, core=0):
        place = 0
        for name in names:
            if name in FRONT:
                here = x if name == "x" else core
            else:
                here = member >> LEAF[::-1].index(name) & 1
            place = place * axes[name] + here
        return place

    def by_front(names, count):
        pairs = [(x, core) for x in range(axes["x"]) for core in range(axes["core"])]
        return [[slot(names, m, *pair) for m in range(count)] for pair in pairs]

    def member_slots(level, member):
        names = GROUP[level]
        xs = range(axes["x"] if "x" in names else 1)
        cores = range(axes["core"] if "core" in names else 1)
        return [slot(names, member, x, core) for x in xs for core in cores]

    def message_count(level):
        return len(member_slots(level, 0)) * (blocks >> (level + 1))

    def first_body(rhs_hbm, sent, rhs_ref, sem):
        move = pltpu.make_async_copy(rhs_hbm, rhs_ref, sem)
        move.start()
        move.wait()
        put(sent, range(fronts), packing.pack(both_parts(rhs_ref, levels - 1)))

    def same(array):
        return jax.ShapeDtypeStruct(array.shape, array.dtype)

    sent, rhs = call(
        first_body,
        (sent_shape(fronts), same(rhs)),
        (pltpu.with_memory_space_constraint(rhs, pltpu.HBM),),
        pltpu.HBM,
        (pltpu.SemaphoreType.DMA(()),),
        pl.CostEstimate(flops=10**10, transcendentals=0, bytes_accessed=2 * 10**7),
    )

    def invert(level, received, order):
        members = blocks >> (level + 1)

        def body(received_ref, matrix, sent):
            block = packing.unpack(summed_chunks(received_ref, order))
            out, shift = products(block, matrix, (blocks - 2 * members) * rows_dev, members * rows_dev)
            for a in range(members):
                lane = shift + a * rows_dev
                strips = packing.pack(out[:, lane : lane + rows_dev])
                put(sent, member_slots(level, a), strips)

        return call(body, sent_shape(message_count(level), WIRE[level]), (received, inv_blocks))

    def update(level, received, order, known):
        members = blocks >> (level + 1)
        offset = blocks // 2 - 2 * members

        def body(mask, received_ref, rhs_ref, matrix, *outs):
            sent = outs[0]
            chunks = summed_chunks(received_ref, order)
            if not known:
                write_solution(outs[1], own_chunk(chunks, lax.axis_index(FRONT)))
            out, shift = products(packing.unpack(chunks), matrix, offset * rows_dev, members * rows_dev)
            own = lax.axis_index(LEAF) % members
            gates = mask[...].astype(jnp.float32)
            right = both_parts(rhs_ref, level - 1)
            for a in range(members):
                lane = shift + a * rows_dev
                part = out[:, lane : lane + rows_dev] * gates[:, offset + a : offset + a + 1]
                strips = packing.pack(jnp.where(own == a, right, 0.0) - part)
                put(sent, member_slots(level, a), strips)

        outs = (sent_shape(message_count(level), WIRE[level]),) + (() if known else (sol_shape,))
        return call(body, outs, (tile_mask, received, rhs, upd_blocks))

    def combine(level, received, solution):
        members = blocks >> (level + 1)
        kept = axes["x"] if "x" in GROUP[level] else 1
        copies = fronts if WAY[level] == THEN_FRONT else 1

        def body(received_ref, sent, *outs):
            chunks = summed_chunks(received_ref, [[slot(GROUP[level], m, k) for m in range(members)] for k in range(kept)])
            if solution:
                own = lax.axis_index("x") if kept > 1 else 0
                write_solution(outs[0], own_chunk(chunks, own))
            for k in range(kept):
                put(sent, range(k * copies, (k + 1) * copies), chunks[k])

        outs = (sent_shape(kept * copies),) + ((sol_shape,) if solution else ())
        return call(body, outs, (received,))

    def exchange(level, sent, solution):
        names = GROUP[level]
        if WAY[level] == WITH_FRONT:
            return over(sent, names), by_front(names, blocks >> (level + 1)), None
        sent, *solved = combine(level, over(sent, names), solution)
        if WAY[level] == THEN_FRONT:
            return over(sent, FRONT), by_front(FRONT, 1), solved[0] if solution else None
        both = lax.all_gather(sent, "core", axis=0, tiled=True)
        return both, by_front(("core", "x"), 1), solved[0] if solution else None

    def finish(received, solved):
        def body(received_ref, *refs):
            out = refs[-1]
            write_solution(out.at[0], summed_chunks(received_ref, [range(received.shape[0])])[0])
            for level in range(1, levels):
                out[level] = refs[level - 1][...]

        return call(body, same(rhs), (received, *solved))

    received, order = over(sent, FRONT), by_front(FRONT, 1)
    solved = [None] * levels
    for level in range(levels - 1, 0, -1):
        received, order, solved[level] = exchange(level, invert(level, received, order), True)
        sent, *rest = update(level, received, order, solved[level] is not None)
        if rest:
            solved[level] = rest[0]
        received, order, _ = exchange(level, sent, False)
    return finish(over(invert(0, received, order), GROUP[0]), solved[1:])


def solution(mesh):
    finer = Mesh(mesh.devices.reshape(2, 2, 2, 2, 2, 2, 4, 2), LEAF + FRONT)
    placed = (
        P(None, None, None, LEAF + FRONT),
        P(None, LEAF, FRONT),
        P(None, LEAF, FRONT),
        P(LEAF, None),
    )
    return jax.shard_map(
        shards,
        mesh=finer,
        in_specs=placed,
        out_specs=P(None, None, None, LEAF + FRONT),
        check_vma=False,
    )
```

```python
import jax
import jax.numpy as jnp
from jax import lax
from jax.experimental import pallas as pl
from jax.experimental.pallas import tpu as pltpu
from jax.sharding import Mesh
from jax.sharding import PartitionSpec as P

LEAF = ("y1", "y0", "z3", "z2", "z1", "z0")
FRONT = ("x", "core")
WITH_FRONT, THEN_FRONT, WITH_X_THEN_CORE = range(3)
WAY = {4: WITH_FRONT, 3: WITH_FRONT, 2: WITH_X_THEN_CORE, 1: THEN_FRONT}
GROUP = {
    4: ("z0", "x", "core"),
    3: ("z0", "x", "core", "z1"),
    2: ("z0", "x", "z1", "z2"),
    1: ("z1", "z2", "z3", "z0"),
    0: ("z3", "z2", "z1", "z0", "y0"),
}
WIDE_INVERSE = (4, 3)
WIDE_UPDATE = (4,)
STRIP = 4


def lane_window(columns, start, width):
    first = start // 128 * 128
    last = min(-(-(start + width) // 128) * 128, columns)
    return first, last


def whole(space=pltpu.VMEM):
    return pl.BlockSpec(memory_space=space)


def call(body, outs, inputs, space=pltpu.VMEM, scratch=(), cost=None):
    return pl.pallas_call(
        body,
        out_shape=outs,
        in_specs=[whole(space)] * len(inputs),
        out_specs=jax.tree.map(lambda _: whole(), outs),
        scratch_shapes=scratch,
        cost_estimate=cost,
        compiler_params=pltpu.CompilerParams(vmem_limit_bytes=16 * 2**20),
    )(*inputs)


class Packing:
    def __init__(self, rows, lanes):
        self.rows, self.lanes = rows, lanes
        self.groups = 128 // lanes
        self.strips = -(-rows // (self.groups * STRIP))
        self.shape = (self.strips, STRIP, self.groups * lanes)

    def first_row(self, group, strip):
        return (group * self.strips + strip) * STRIP

    def pack(self, block):
        strips = []
        for j in range(self.strips):
            pieces = []
            for g in range(self.groups):
                row = self.first_row(g, j)
                if row < self.rows:
                    pieces.append(block[row : row + STRIP])
                else:
                    pieces.append(jnp.zeros((STRIP, self.lanes), jnp.float32))
            strips.append(jnp.concatenate(pieces, axis=1))
        return strips

    def unpack(self, chunks):
        rows = []
        for g in range(self.groups):
            for j in range(self.strips):
                if self.first_row(g, j) < self.rows:
                    low = g * self.lanes
                    rows.append(jnp.concatenate([c[j][:, low : low + self.lanes] for c in chunks], axis=1))
        return jnp.concatenate(rows, axis=0)


def summed_chunks(received, order):
    chunks = []
    for messages in order:
        strips = []
        for j in range(received.shape[1]):
            total = received[messages[0], j].astype(jnp.float32)
            for m in messages[1:]:
                total = total + received[m, j].astype(jnp.float32)
            strips.append(total)
        chunks.append(strips)
    return chunks


def own_chunk(chunks, own):
    strips = []
    for j in range(len(chunks[0])):
        total = jnp.zeros(chunks[0][j].shape, jnp.float32)
        for c in range(len(chunks)):
            total = total + jnp.where(own == c, chunks[c][j], 0.0)
        strips.append(total)
    return strips


def products(block, matrix, start, width):
    half = block.shape[0] // 2
    real, imag = block[:half], block[half:]
    upper = jnp.concatenate([real, -imag], axis=1)
    lower = jnp.concatenate([imag, real], axis=1)
    stacked = jnp.concatenate([upper, lower], axis=0).astype(jnp.bfloat16)
    first, last = lane_window(matrix.shape[2], start, width)
    weights = matrix[:, :, first:last].reshape(-1, last - first)
    return jnp.dot(stacked, weights, preferred_element_type=jnp.float32), start - first


def put(sent, slots, strips):
    for j, strip in enumerate(strips):
        value = strip.astype(sent.dtype)
        for slot in slots:
            sent[slot, j] = value


def shards(rhs, inv_blocks, upd_blocks, tile_mask):
    axes = {name: lax.axis_size(name) for name in LEAF + FRONT}
    fronts = axes["x"] * axes["core"]
    blocks = 1
    for name in LEAF:
        blocks *= axes[name]
    levels, _, rhs_count, rows_dev = rhs.shape
    packing = Packing(2 * rhs_count, rows_dev)

    def wire(wide):
        return jnp.float32 if wide else jnp.bfloat16

    def sent_shape(count, dtype=jnp.bfloat16):
        return jax.ShapeDtypeStruct((count,) + packing.shape, dtype)

    sol_shape = jax.ShapeDtypeStruct((2, rhs_count, rows_dev), jnp.float32)

    def both_parts(rhs_ref, level):
        return jnp.concatenate([rhs_ref[level, 0], rhs_ref[level, 1]], axis=0)

    def write_solution(sol, strips):
        value = packing.unpack([strips])
        sol[0] = value[:rhs_count]
        sol[1] = value[rhs_count:]

    def over(value, names):
        return lax.all_to_all(value, names, 0, 0, tiled=True)

    def slot(names, member, x=0, core=0):
        place = 0
        for name in names:
            if name in FRONT:
                here = x if name == "x" else core
            else:
                here = member >> LEAF[::-1].index(name) & 1
            place = place * axes[name] + here
        return place

    def by_front(names, count):
        pairs = [(x, core) for x in range(axes["x"]) for core in range(axes["core"])]
        return [[slot(names, m, *pair) for m in range(count)] for pair in pairs]

    def member_slots(level, member):
        names = GROUP[level]
        xs = range(axes["x"] if "x" in names else 1)
        cores = range(axes["core"] if "core" in names else 1)
        return [slot(names, member, x, core) for x in xs for core in cores]

    def message_count(level):
        return len(member_slots(level, 0)) * (blocks >> (level + 1))

    def first_body(rhs_hbm, sent, rhs_ref, sem):
        move = pltpu.make_async_copy(rhs_hbm, rhs_ref, sem)
        move.start()
        move.wait()
        put(sent, range(fronts), packing.pack(both_parts(rhs_ref, levels - 1)))

    def same(array):
        return jax.ShapeDtypeStruct(array.shape, array.dtype)

    sent, rhs = call(
        first_body,
        (sent_shape(fronts), same(rhs)),
        (pltpu.with_memory_space_constraint(rhs, pltpu.HBM),),
        pltpu.HBM,
        (pltpu.SemaphoreType.DMA(()),),
        pl.CostEstimate(flops=10**10, transcendentals=0, bytes_accessed=2 * 10**7),
    )

    def invert(level, received, order):
        members = blocks >> (level + 1)

        def body(received_ref, matrix, sent):
            block = packing.unpack(summed_chunks(received_ref, order))
            out, shift = products(block, matrix, (blocks - 2 * members) * rows_dev, members * rows_dev)
            for a in range(members):
                lane = shift + a * rows_dev
                strips = packing.pack(out[:, lane : lane + rows_dev])
                put(sent, member_slots(level, a), strips)

        return call(body, sent_shape(message_count(level), wire(level in WIDE_INVERSE)), (received, inv_blocks))

    def update(level, received, order, known):
        members = blocks >> (level + 1)
        offset = blocks // 2 - 2 * members

        def body(mask, received_ref, rhs_ref, matrix, *outs):
            sent = outs[0]
            chunks = summed_chunks(received_ref, order)
            if not known:
                write_solution(outs[1], own_chunk(chunks, lax.axis_index(FRONT)))
            out, shift = products(packing.unpack(chunks), matrix, offset * rows_dev, members * rows_dev)
            own = lax.axis_index(LEAF) % members
            gates = mask[...].astype(jnp.float32)
            right = both_parts(rhs_ref, level - 1)
            for a in range(members):
                lane = shift + a * rows_dev
                part = out[:, lane : lane + rows_dev] * gates[:, offset + a : offset + a + 1]
                strips = packing.pack(jnp.where(own == a, right, 0.0) - part)
                put(sent, member_slots(level, a), strips)

        outs = (sent_shape(message_count(level), wire(level in WIDE_UPDATE)),) + (() if known else (sol_shape,))
        return call(body, outs, (tile_mask, received, rhs, upd_blocks))

    def combine(level, received, solution):
        members = blocks >> (level + 1)
        kept = axes["x"] if "x" in GROUP[level] else 1
        copies = fronts if WAY[level] == THEN_FRONT else 1

        def body(received_ref, sent, *outs):
            chunks = summed_chunks(received_ref, [[slot(GROUP[level], m, k) for m in range(members)] for k in range(kept)])
            if solution:
                own = lax.axis_index("x") if kept > 1 else 0
                write_solution(outs[0], own_chunk(chunks, own))
            for k in range(kept):
                put(sent, range(k * copies, (k + 1) * copies), chunks[k])

        outs = (sent_shape(kept * copies),) + ((sol_shape,) if solution else ())
        return call(body, outs, (received,))

    def exchange(level, sent, solution):
        names = GROUP[level]
        if WAY[level] == WITH_FRONT:
            return over(sent, names), by_front(names, blocks >> (level + 1)), None
        sent, *solved = combine(level, over(sent, names), solution)
        if WAY[level] == THEN_FRONT:
            return over(sent, FRONT), by_front(FRONT, 1), solved[0] if solution else None
        both = lax.all_gather(sent, "core", axis=0, tiled=True)
        return both, by_front(("core", "x"), 1), solved[0] if solution else None

    def finish(received, solved):
        def body(received_ref, *refs):
            out = refs[-1]
            write_solution(out.at[0], summed_chunks(received_ref, [range(received.shape[0])])[0])
            for level in range(1, levels):
                out[level] = refs[level - 1][...]

        return call(body, same(rhs), (received, *solved))

    received, order = over(sent, FRONT), by_front(FRONT, 1)
    solved = [None] * levels
    for level in range(levels - 1, 0, -1):
        received, order, solved[level] = exchange(level, invert(level, received, order), True)
        sent, *rest = update(level, received, order, solved[level] is not None)
        if rest:
            solved[level] = rest[0]
        received, order, _ = exchange(level, sent, False)
    return finish(over(invert(0, received, order), GROUP[0]), solved[1:])


def solution(mesh):
    finer = Mesh(mesh.devices.reshape(2, 2, 2, 2, 2, 2, 4, 2), LEAF + FRONT)
    placed = (
        P(None, None, None, LEAF + FRONT),
        P(None, LEAF, FRONT),
        P(None, LEAF, FRONT),
        P(LEAF, None),
    )
    return jax.shard_map(
        shards,
        mesh=finer,
        in_specs=placed,
        out_specs=P(None, None, None, LEAF + FRONT),
        check_vma=False,
    )
```

```python
import jax
import jax.numpy as jnp
from jax import lax
from jax.experimental import pallas as pl
from jax.experimental.pallas import tpu as pltpu
from jax.sharding import Mesh
from jax.sharding import PartitionSpec as P

LEAF = ("y1", "y0", "z3", "z2", "z1", "z0")
FRONT = ("x", "core")
WITH_FRONT, THEN_FRONT, WITH_X_THEN_CORE = range(3)
WAY = {4: WITH_FRONT, 3: WITH_FRONT, 2: WITH_X_THEN_CORE, 1: THEN_FRONT}
GROUP = {
    4: ("z0", "x", "core"),
    3: ("z0", "x", "core", "z1"),
    2: ("z0", "x", "z1", "z2"),
    1: ("z1", "z2", "z3", "z0"),
    0: ("z3", "z2", "z1", "z0", "y0"),
}
WIDE_INVERSE = (4, 3)
WIDE_UPDATE = (4,)
STRIP = 4


def lane_window(columns, start, width):
    first = start // 128 * 128
    last = min(-(-(start + width) // 128) * 128, columns)
    return first, last


def whole(space=pltpu.VMEM):
    return pl.BlockSpec(memory_space=space)


def call(body, outs, inputs, space=pltpu.VMEM, scratch=(), cost=None):
    return pl.pallas_call(
        body,
        out_shape=outs,
        in_specs=[whole(space)] * len(inputs),
        out_specs=jax.tree.map(lambda _: whole(), outs),
        scratch_shapes=scratch,
        cost_estimate=cost,
        compiler_params=pltpu.CompilerParams(vmem_limit_bytes=16 * 2**20),
    )(*inputs)


class Packing:
    def __init__(self, rows, lanes):
        self.rows, self.lanes = rows, lanes
        self.groups = 128 // lanes
        self.strips = -(-rows // (self.groups * STRIP))
        self.shape = (self.strips, STRIP, self.groups * lanes)

    def first_row(self, group, strip):
        return (group * self.strips + strip) * STRIP

    def pack(self, block):
        strips = []
        for j in range(self.strips):
            pieces = []
            for g in range(self.groups):
                row = self.first_row(g, j)
                if row < self.rows:
                    pieces.append(block[row : row + STRIP])
                else:
                    pieces.append(jnp.zeros((STRIP, self.lanes), jnp.float32))
            strips.append(jnp.concatenate(pieces, axis=1))
        return strips

    def unpack(self, chunks):
        rows = []
        for g in range(self.groups):
            for j in range(self.strips):
                if self.first_row(g, j) < self.rows:
                    low = g * self.lanes
                    rows.append(jnp.concatenate([c[j][:, low : low + self.lanes] for c in chunks], axis=1))
        return jnp.concatenate(rows, axis=0)


def summed_chunks(received, order):
    chunks = []
    for messages in order:
        strips = []
        for j in range(received.shape[1]):
            total = received[messages[0], j].astype(jnp.float32)
            for m in messages[1:]:
                total = total + received[m, j].astype(jnp.float32)
            strips.append(total)
        chunks.append(strips)
    return chunks


def own_chunk(chunks, own):
    strips = []
    for j in range(len(chunks[0])):
        total = jnp.zeros(chunks[0][j].shape, jnp.float32)
        for c in range(len(chunks)):
            total = total + jnp.where(own == c, chunks[c][j], 0.0)
        strips.append(total)
    return strips


def products(block, matrix, start, width):
    half = block.shape[0] // 2
    real, imag = block[:half], block[half:]
    upper = jnp.concatenate([real, -imag], axis=1)
    lower = jnp.concatenate([imag, real], axis=1)
    stacked = jnp.concatenate([upper, lower], axis=0).astype(jnp.bfloat16)
    first, last = lane_window(matrix.shape[2], start, width)
    weights = matrix[:, :, first:last].reshape(-1, last - first)
    return jnp.dot(stacked, weights, preferred_element_type=jnp.float32), start - first


def put(sent, slots, strips):
    for j, strip in enumerate(strips):
        value = strip.astype(sent.dtype)
        for slot in slots:
            sent[slot, j] = value


def shards(rhs, inv_blocks, upd_blocks, tile_mask):
    axes = {name: lax.axis_size(name) for name in LEAF + FRONT}
    fronts = axes["x"] * axes["core"]
    blocks = 1
    for name in LEAF:
        blocks *= axes[name]
    levels, _, rhs_count, rows_dev = rhs.shape
    packing = Packing(2 * rhs_count, rows_dev)

    def wire(wide):
        return jnp.float32 if wide else jnp.bfloat16

    def sent_shape(count, dtype=jnp.bfloat16):
        return jax.ShapeDtypeStruct((count,) + packing.shape, dtype)

    sol_shape = jax.ShapeDtypeStruct((2, rhs_count, rows_dev), jnp.float32)

    def both_parts(rhs_ref, level):
        return jnp.concatenate([rhs_ref[level, 0], rhs_ref[level, 1]], axis=0)

    def write_solution(sol, strips):
        value = packing.unpack([strips])
        sol[0] = value[:rhs_count]
        sol[1] = value[rhs_count:]

    def over(value, names):
        return lax.all_to_all(value, names, 0, 0, tiled=True)

    def slot(names, member, x=0, core=0):
        place = 0
        for name in names:
            if name in FRONT:
                here = x if name == "x" else core
            else:
                here = member >> LEAF[::-1].index(name) & 1
            place = place * axes[name] + here
        return place

    def by_front(names, count):
        pairs = [(x, core) for x in range(axes["x"]) for core in range(axes["core"])]
        return [[slot(names, m, *pair) for m in range(count)] for pair in pairs]

    def member_slots(level, member):
        names = GROUP[level]
        xs = range(axes["x"] if "x" in names else 1)
        cores = range(axes["core"] if "core" in names else 1)
        return [slot(names, member, x, core) for x in xs for core in cores]

    def message_count(level):
        return len(member_slots(level, 0)) * (blocks >> (level + 1))

    def first_body(rhs_hbm, sent, rhs_ref, sem):
        move = pltpu.make_async_copy(rhs_hbm, rhs_ref, sem)
        move.start()
        move.wait()
        put(sent, range(fronts), packing.pack(both_parts(rhs_ref, levels - 1)))

    def same(array):
        return jax.ShapeDtypeStruct(array.shape, array.dtype)

    sent, rhs = call(
        first_body,
        (sent_shape(fronts), same(rhs)),
        (pltpu.with_memory_space_constraint(rhs, pltpu.HBM),),
        pltpu.HBM,
        (pltpu.SemaphoreType.DMA(()),),
        pl.CostEstimate(flops=10**10, transcendentals=0, bytes_accessed=2 * 10**7),
    )

    def invert(level, received, order):
        members = blocks >> (level + 1)

        def body(received_ref, matrix, sent):
            block = packing.unpack(summed_chunks(received_ref, order))
            out, shift = products(block, matrix, (blocks - 2 * members) * rows_dev, members * rows_dev)
            for a in range(members):
                lane = shift + a * rows_dev
                strips = packing.pack(out[:, lane : lane + rows_dev])
                put(sent, member_slots(level, a), strips)

        return call(body, sent_shape(message_count(level), wire(level in WIDE_INVERSE)), (received, inv_blocks))

    def update(level, received, order, known):
        members = blocks >> (level + 1)
        offset = blocks // 2 - 2 * members

        def body(mask, received_ref, rhs_ref, matrix, *outs):
            sent = outs[0]
            chunks = summed_chunks(received_ref, order)
            if not known:
                write_solution(outs[1], own_chunk(chunks, lax.axis_index(FRONT)))
            out, shift = products(packing.unpack(chunks), matrix, offset * rows_dev, members * rows_dev)
            own = lax.axis_index(LEAF) % members
            gates = mask[...].astype(jnp.float32)
            right = both_parts(rhs_ref, level - 1)
            for a in range(members):
                lane = shift + a * rows_dev
                part = out[:, lane : lane + rows_dev] * gates[:, offset + a : offset + a + 1]
                strips = packing.pack(jnp.where(own == a, right, 0.0) - part)
                put(sent, member_slots(level, a), strips)

        outs = (sent_shape(message_count(level), wire(level in WIDE_UPDATE)),) + (() if known else (sol_shape,))
        return call(body, outs, (tile_mask, received, rhs, upd_blocks))

    def combine(level, received, solution):
        members = blocks >> (level + 1)
        kept = axes["x"] if "x" in GROUP[level] else 1
        copies = fronts if WAY[level] == THEN_FRONT else 1

        def body(received_ref, sent, *outs):
            chunks = summed_chunks(received_ref, [[slot(GROUP[level], m, k) for m in range(members)] for k in range(kept)])
            if solution:
                own = lax.axis_index("x") if kept > 1 else 0
                write_solution(outs[0], own_chunk(chunks, own))
            for k in range(kept):
                put(sent, range(k * copies, (k + 1) * copies), chunks[k])

        outs = (sent_shape(kept * copies),) + ((sol_shape,) if solution else ())
        return call(body, outs, (received,))

    def exchange(level, sent, solution):
        names = GROUP[level]
        if WAY[level] == WITH_FRONT:
            return over(sent, names), by_front(names, blocks >> (level + 1)), None
        sent, *solved = combine(level, over(sent, names), solution)
        if WAY[level] == THEN_FRONT:
            return over(sent, FRONT[::-1]), by_front(FRONT[::-1], 1), solved[0] if solution else None
        both = lax.all_gather(sent, "core", axis=0, tiled=True)
        return both, by_front(("core", "x"), 1), solved[0] if solution else None

    def finish(received, solved):
        def body(received_ref, *refs):
            out = refs[-1]
            write_solution(out.at[0], summed_chunks(received_ref, [range(received.shape[0])])[0])
            for level in range(1, levels):
                out[level] = refs[level - 1][...]

        return call(body, same(rhs), (received, *solved))

    received, order = over(sent, FRONT[::-1]), by_front(FRONT[::-1], 1)
    solved = [None] * levels
    for level in range(levels - 1, 0, -1):
        received, order, solved[level] = exchange(level, invert(level, received, order), True)
        sent, *rest = update(level, received, order, solved[level] is not None)
        if rest:
            solved[level] = rest[0]
        received, order, _ = exchange(level, sent, False)
    return finish(over(invert(0, received, order), GROUP[0]), solved[1:])


def solution(mesh):
    finer = Mesh(mesh.devices.reshape(2, 2, 2, 2, 2, 2, 4, 2), LEAF + FRONT)
    placed = (
        P(None, None, None, LEAF + FRONT),
        P(None, LEAF, FRONT),
        P(None, LEAF, FRONT),
        P(LEAF, None),
    )
    return jax.shard_map(
        shards,
        mesh=finer,
        in_specs=placed,
        out_specs=P(None, None, None, LEAF + FRONT),
        check_vma=False,
    )
```
